256 devices in a mesh: ctx: 32 (over y_lo, z, core), exp: 8 (over y_hi, x).
Axes of the slice: x: 4, y: 4 (y_hi: 2, y_lo: 2; y = y_hi * 2 + y_lo), z: 8, core: 2. Of those that a mesh axis runs over, the one named last changes fastest.
Arguments:
- query: bfloat16 [8, 4096, 2048], P('exp', 'ctx'), may hold values from -12 to 12
- key: bfloat16 [8, 4096, 2048], P('exp', 'ctx'), may hold values from -6 to 6
- value: bfloat16 [8, 4096, 2048], P('exp', 'ctx'), may hold values from -12 to 12
- cotangent: bfloat16 [8, 4096, 2048], P('exp', 'ctx'), may hold values from -6 to 6
- route_ids: int32 [8, 4096, 1], P('exp', 'ctx'), may hold values from 0 to 7; in each aligned block of 128 rows (0 to 127, 128 to 255, ..., all dimensions but the last counted through in order) at most 32 rows name the same one
- route_weights: float32 [8, 4096, 1], P('exp', 'ctx'), may hold values from 0.2 to 1
- block_mask: int32 [8, 32, 3], P('exp', 'ctx'), may hold values 0 or 1
- w_gate: bfloat16 [8, 2048, 512], P('exp'), may hold values from -0.125 to 0.125
- w_up: bfloat16 [8, 2048, 512], P('exp'), may hold values from -0.125 to 0.125
- w_down: bfloat16 [8, 512, 2048], P('exp'), may hold values from -0.25 to 0.25
Outputs:
- layer_out: bfloat16 [8, 4096, 2048], P('exp', 'ctx')
- grad_query: bfloat16 [8, 4096, 2048], P('exp', 'ctx')
- grad_key: bfloat16 [8, 4096, 2048], P('exp', 'ctx')
- grad_value: bfloat16 [8, 4096, 2048], P('exp', 'ctx')
- tangent_out: bfloat16 [8, 4096, 2048], P('exp', 'ctx')
The draws below stay inside these ranges and needn't reach their ends.
Inputs may be any that keep to these rules, and one draw needn't show every extreme that they name: `route_ids`: among the 128 tokens of one block of a sequence, the routes of a token name distinct experts, no expert is named by more than 32 routes, and in every draw some block names some expert exactly 32 times.
All inputs are finite; a program needn't handle non-finite values. No bound on the sum of `block_mask` on one device may be relied on, other than what follows from the above.
Results may differ from the reference program's by a relative error of at most 0.035.
Values may be sent and summed in bfloat16 or wider, within the bound.
A program may use at most 128 MiB of HBM per device.

```python
import math
import jax
import jax.numpy as jnp
import numpy as np
from jax import lax

D = 2048
HEADS = 16
FFH = 512
TOK_DEV = 128
WIN = 4
EXPERTS = 8
TOPK = 1
CAP = 32
LEN = 4096
SEQS = 8
N_CTX = 32


def plant_plan(key):
    base_key = jax.random.fold_in(key, 901)
    block_count = SEQS * (LEN // TOK_DEV)
    head_size = D // HEADS
    key_rows, key_heads, key_signs, key_gaps = jax.random.split(base_key, 4)
    plant_rows = jax.random.randint(key_rows, (block_count,), 1, TOK_DEV)
    plant_heads = jax.random.randint(key_heads, (block_count,), 0, HEADS)
    plant_signs = (jax.random.randint(key_signs, (block_count, head_size), 0, 2) * 2 - 1).astype(jnp.float32)
    plant_gaps = jax.random.uniform(key_gaps, (block_count,), jnp.float32, 1.5, 2.5)
    cycle = jnp.arange(block_count, dtype=jnp.int32) % 3
    strengths = jnp.where(cycle == 0, 1.75, jnp.where(cycle == 1, 2.5, 3.5)).astype(jnp.float32)
    return (plant_rows, plant_heads, plant_signs, plant_gaps, strengths)


def base_field(key, spread, limit):
    noise_key = jax.random.fold_in(key, 902)
    field = jnp.clip(jax.random.normal(noise_key, (SEQS, LEN, D), jnp.float32) * spread, -limit, limit)
    return field.reshape(SEQS * (LEN // TOK_DEV), TOK_DEV, HEADS, D // HEADS)


def head_mask(plant_heads):
    return (jnp.arange(HEADS, dtype=jnp.int32)[None, :] == plant_heads[:, None])[:, None, :, None]


def draw_query(key, part):
    plant_rows, plant_heads, plant_signs, plant_gaps, strengths = plant_plan(key)
    field = base_field(jax.random.fold_in(key, 11), 2.0, 12.0)
    row_hit = (jnp.arange(TOK_DEV, dtype=jnp.int32)[None, :] == plant_rows[:, None])[:, :, None, None]
    planted = strengths[:, None, None, None] * plant_signs[:, None, None, :]
    field = jnp.where(row_hit & head_mask(plant_heads), planted, field)
    return field.reshape(SEQS, LEN, D).astype(jnp.bfloat16)


def draw_key(key, part):
    plant_rows, plant_heads, plant_signs, plant_gaps, strengths = plant_plan(key)
    field = base_field(jax.random.fold_in(key, 13), 1.0, 6.0)
    head_size = D // HEADS
    rowpos = jnp.arange(TOK_DEV, dtype=jnp.int32)[None, :]
    top_hit = (rowpos == plant_rows[:, None])[:, :, None, None]
    next_hit = (rowpos == plant_rows[:, None] - 1)[:, :, None, None]
    lowered = (jnp.arange(head_size, dtype=jnp.int32) < 4)[None, :]
    drop = plant_gaps * head_size ** 0.5 / (strengths * 4.0)
    first_key = 6.0 * plant_signs
    second_key = plant_signs * (6.0 - jnp.where(lowered, drop[:, None], 0.0))
    in_head = head_mask(plant_heads)
    field = jnp.where(top_hit & in_head, first_key[:, None, None, :], field)
    field = jnp.where(next_hit & in_head, second_key[:, None, None, :], field)
    return field.reshape(SEQS, LEN, D).astype(jnp.bfloat16)


def set_ends(entries, key, low, top_value):
    longest = entries.shape.index(max(entries.shape))
    spots = []
    for shift in (0, 1):
        where = [jax.random.randint(jax.random.fold_in(key, axis), (), 0, length) for axis, length in enumerate(entries.shape)]
        where[longest] = (where[longest] + shift) % entries.shape[longest]
        spots.append(tuple(where))
    return entries.at[spots[0]].set(low).at[spots[1]].set(top_value)


def block_scale(own_key, dims, cuts, smallest, high):
    def one(axis_at, blocks):
        draws = jax.random.uniform(jax.random.fold_in(jax.random.fold_in(own_key, 6), axis_at), (blocks,), jnp.float32, smallest / len(cuts), high / len(cuts))
        return jnp.repeat(jnp.exp(draws), dims[axis_at] // blocks).reshape((-1,) + (1,) * (len(dims) - axis_at - 1))

    level = one(*cuts[0])
    for cut in cuts[1:]:
        level = level * one(*cut)
    return level


def deal_out(key, own, number, rows, amount, top, bound, lean):
    ranking = jax.random.permutation(key, amount)
    heavy_load, common = shares(amount, rows * top, bound, lean, True), shares(amount, rows * top, bound, lean, False)
    places = jnp.arange(amount)

    def named(tallies, offset_by):
        used = int((tallies > 0).sum())
        fixed = max(1, used // 4)
        moved = fixed + (places - fixed + offset_by * (used - fixed)) % max(1, amount - fixed)
        return jnp.zeros((amount,), jnp.int32).at[ranking[jnp.where(places < fixed, places, moved)]].set(jnp.asarray(tallies, jnp.int32))

    tallies = jnp.where(number % 4 == 0, named(heavy_load, number // 4), named(common, number - number // 4 - 1))
    mixed = jax.random.permutation(jax.random.fold_in(own, 3), amount)
    giver, taker = mixed[0:amount // 2 * 2:2], mixed[1:amount // 2 * 2:2]
    margin = jnp.minimum(tallies[giver] - 1, bound - tallies[taker]) // 2
    margin = jnp.where((giver == ranking[0]) | (taker == ranking[0]) | (tallies[taker] == 0), 0, jnp.maximum(margin, 0))
    moved = jax.random.randint(jax.random.fold_in(own, 4), (amount // 2,), 0, 1 << 20) % (margin + 1)
    tallies = tallies.at[giver].add(-moved).at[taker].add(moved)
    labels = jnp.searchsorted(jnp.cumsum(tallies), jnp.arange(rows * top), side="right").astype(jnp.int32)
    grid = labels.reshape(top, rows).T
    grid = grid[jax.random.permutation(jax.random.fold_in(own, 1), rows)]
    offset_by = jax.random.randint(jax.random.fold_in(own, 2), (rows, 1), 0, top)
    return jnp.take_along_axis(grid, (jnp.arange(top)[None, :] + offset_by) % top, axis=1)


def shares(number_of, total, most, lean, full):
    loads = [(1 << 20) // math.isqrt(standing ** lean) + 1 for standing in range(1, number_of + 1)]
    largest = most if full else min(most, max(-(-total // number_of), total * loads[0] // sum(loads)))
    least = 1 if total - largest >= number_of - 1 else 0
    given, rest = [largest] + [least] * (number_of - 1), total - largest - least * (number_of - 1)
    while rest > 0:
        movable = [i for i in range(1, number_of) if given[i] < largest] or [i for i in range(1, number_of) if given[i] < most]
        pool, left = sum([loads[i] for i in movable]), rest
        for i in movable:
            more = min(most - given[i], max(1, left * loads[i] // pool), rest)
            given[i] = given[i] + more
            rest = rest - more
    return np.array(given)


def gaussian(key, dims, deviation, reach, shards=(), kind=jnp.bfloat16):
    entries = jax.random.normal(key, dims, jnp.float32) * deviation
    if len(shards) > 0:
        entries = block_scale(key, dims, shards, -0.22, 0.18) * entries
    return jnp.clip(entries, min=-reach, max=reach).astype(kind)


def setup_inputs(seed: int = 0) -> dict:
    streams_of = jax.random.split(jax.random.key(seed), 11)
    query = draw_query(jax.random.fold_in(streams_of[10], 71), 0)
    key = draw_key(jax.random.fold_in(streams_of[10], 71), 0)
    value = gaussian(streams_of[2], (SEQS, LEN, D), 2.0, 12.0, ((0, 8), (1, 32)))
    cotangent = gaussian(streams_of[3], (SEQS, LEN, D), 1.0, 6.0, ((0, 8), (1, 32)))
    route_ids_keys = jax.random.split(jax.random.fold_in(streams_of[4], 1), SEQS * LEN // TOK_DEV)
    route_ids_turns = jax.random.permutation(jax.random.fold_in(streams_of[4], 3), SEQS * LEN // TOK_DEV)
    route_ids = jax.vmap(lambda own, number: deal_out(jax.random.fold_in(streams_of[4], 2), own, number, TOK_DEV, EXPERTS, TOPK, CAP, 2))(route_ids_keys, route_ids_turns).reshape((SEQS, LEN, TOPK))
    route_weights = jnp.clip(0.2 + 0.8 * jax.random.uniform(streams_of[5], (SEQS, LEN, TOPK), jnp.float32) ** block_scale(streams_of[5], (SEQS, LEN, TOPK), ((0, 8), (1, 32)), -0.2, 0.2), 0.2, 1.0)
    block_mask = set_ends((jax.random.randint(streams_of[6], (SEQS, N_CTX, WIN - 1), 0, 4) < 3).astype(jnp.int32), jax.random.fold_in(streams_of[6], 1), 0, 1)
    w_gate = gaussian(streams_of[7], (EXPERTS, D, FFH), D ** -0.5, 0.125, ((0, 8),))
    w_up = gaussian(streams_of[8], (EXPERTS, D, FFH), D ** -0.5, 0.125, ((0, 8),))
    w_down = gaussian(streams_of[9], (EXPERTS, FFH, D), FFH ** -0.5, 0.25, ((0, 8),))
    return dict(query=query, key=key, value=value, cotangent=cotangent, route_ids=route_ids, route_weights=route_weights, block_mask=block_mask, w_gate=w_gate, w_up=w_up, w_down=w_down)


tile_rows = 256


def silu_parts(gate_pre):
    sigmoid_val = jax.nn.sigmoid(gate_pre)
    return gate_pre * sigmoid_val, sigmoid_val * (1.0 + gate_pre * (1.0 - sigmoid_val))


def split_rows(row_block):
    return row_block.astype(jnp.float32).reshape(row_block.shape[0], HEADS, D // HEADS)


def rounded(values_f32):
    return lax.optimization_barrier(values_f32.astype(jnp.bfloat16)).astype(jnp.float32)


def take_block(whole, sequence, block_index):
    start = (block_index * TOK_DEV).astype(jnp.int32)
    return lax.dynamic_slice(whole, (sequence.astype(jnp.int32), start, jnp.int32(0)), (1, TOK_DEV, whole.shape[2]))[0]


def window_of(whole, sequence, block_index):
    return jnp.concatenate([take_block(whole, sequence, jnp.maximum(block_index - offset, 0)) for offset in range(WIN)], axis=0)


def allowed_of(block_mask, sequence, block_index):
    rowpos = jnp.arange(TOK_DEV, dtype=jnp.int32)
    pieces = [rowpos[:, None] >= rowpos[None, :]]
    for offset in range(1, WIN):
        mask_entry = lax.dynamic_slice(block_mask, (sequence.astype(jnp.int32), block_index.astype(jnp.int32), jnp.int32(offset - 1)), (1, 1, 1))[0, 0, 0]
        visible = (block_index >= offset) & (mask_entry == 1)
        pieces.append(jnp.broadcast_to(visible, (TOK_DEV, TOK_DEV)))
    return jnp.concatenate(pieces, axis=1)


def probs_of(query_rows, key_window, allowed):
    scores = jnp.einsum('qhd,khd->hqk', split_rows(query_rows), split_rows(key_window)) * ((D // HEADS) ** -0.5)
    scores = jnp.where(allowed[None], scores, -1e30)
    row_top = jnp.max(scores, axis=-1, keepdims=True)
    exp_scores = jnp.exp(scores - row_top)
    return exp_scores / jnp.sum(exp_scores, axis=-1, keepdims=True)


def expert_forward(row_block, gate_matrix, up_matrix, down_matrix):
    gate_pre = jnp.dot(row_block, gate_matrix, preferred_element_type=jnp.float32)
    up_value = jnp.dot(row_block, up_matrix, preferred_element_type=jnp.float32)
    activated, slope_val = silu_parts(gate_pre)
    hidden = (activated * up_value).astype(jnp.bfloat16)
    return jnp.dot(hidden, down_matrix, preferred_element_type=jnp.float32).astype(jnp.bfloat16), gate_pre, up_value


def expert_backward(cot_block, gate_pre, up_value, gate_matrix, up_matrix, down_matrix):
    hidden_grad = jnp.dot(cot_block, down_matrix.T, preferred_element_type=jnp.float32)
    activated, slope_val = silu_parts(gate_pre)
    gate_grad = (hidden_grad * up_value * slope_val).astype(jnp.bfloat16)
    up_grad = (hidden_grad * activated).astype(jnp.bfloat16)
    summed = jnp.dot(gate_grad, gate_matrix.T, preferred_element_type=jnp.float32) + jnp.dot(up_grad, up_matrix.T, preferred_element_type=jnp.float32)
    return summed.astype(jnp.bfloat16)


def expert_tangent(tan_block, gate_pre, up_value, gate_matrix, up_matrix, down_matrix):
    gate_tan = jnp.dot(tan_block, gate_matrix, preferred_element_type=jnp.float32)
    up_tan = jnp.dot(tan_block, up_matrix, preferred_element_type=jnp.float32)
    activated, slope_val = silu_parts(gate_pre)
    hidden_tan = (slope_val * gate_tan * up_value + activated * up_tan).astype(jnp.bfloat16)
    return jnp.dot(hidden_tan, down_matrix, preferred_element_type=jnp.float32).astype(jnp.bfloat16)


def expert_pass(route_ids, row_sets, w_gate, w_up, w_down, tile_fn):
    flat_ids = route_ids.reshape(-1).astype(jnp.int32)
    pair_count = flat_ids.shape[0]
    sort_order = jnp.argsort(flat_ids, stable=True).astype(jnp.int32)
    sorted_ids = flat_ids[sort_order]
    counts = jnp.sum((flat_ids[:, None] == jnp.arange(EXPERTS, dtype=jnp.int32)[None, :]).astype(jnp.int32), axis=0).astype(jnp.int32)
    starts = (jnp.cumsum(counts) - counts).astype(jnp.int32)
    padded = ((counts + tile_rows - 1) // tile_rows * tile_rows).astype(jnp.int32)
    pad_ends = jnp.cumsum(padded).astype(jnp.int32)
    pad_starts = (pad_ends - padded).astype(jnp.int32)
    positions = (pad_starts[sorted_ids] + jnp.arange(pair_count, dtype=jnp.int32) - starts[sorted_ids]).astype(jnp.int32)
    tile_count = (pair_count + tile_rows - 1) // tile_rows + EXPERTS
    source = jnp.full((tile_count * tile_rows,), pair_count, jnp.int32).at[positions].set(sort_order)
    tile_starts = jnp.arange(tile_count, dtype=jnp.int32) * tile_rows
    tile_expert = jnp.minimum(jnp.sum((tile_starts[:, None] >= pad_ends[None, :]).astype(jnp.int32), axis=1), EXPERTS - 1).astype(jnp.int32)
    stacks = []
    for row_set in row_sets:
        extended = jnp.concatenate([row_set, jnp.zeros((1, row_set.shape[1]), row_set.dtype)], axis=0)
        stacks.append(extended[source].reshape(tile_count, tile_rows, row_set.shape[1]))

    def run_tile(operands):
        expert = operands[0]
        return tile_fn(operands[1:], w_gate[expert], w_up[expert], w_down[expert])

    tile_outs = lax.map(run_tile, (tile_expert,) + tuple(stacks))
    results = []
    for result in tile_outs:
        flattened = result.reshape(tile_count * tile_rows, result.shape[-1])
        results.append(jnp.zeros((pair_count + 1, flattened.shape[1]), flattened.dtype).at[source].set(flattened)[:pair_count])
    return results


def reference(query, key, value, cotangent, route_ids, route_weights, block_mask, w_gate, w_up, w_down):
    score_scale = (D // HEADS) ** -0.5
    blocks = jnp.arange(SEQS * N_CTX, dtype=jnp.int32)

    def forward_block(block):
        sequence = block // N_CTX
        block_index = block % N_CTX
        attn_probs = probs_of(take_block(query, sequence, block_index), window_of(key, sequence, block_index), allowed_of(block_mask, sequence, block_index))
        out_rows = jnp.einsum('hqk,khd->qhd', rounded(attn_probs), split_rows(window_of(value, sequence, block_index)))
        return out_rows.reshape(TOK_DEV, D).astype(jnp.bfloat16)

    attended = lax.map(forward_block, blocks).reshape(SEQS, LEN, D)
    att_rows = attended.reshape(-1, D)
    cot_rows = cotangent.reshape(-1, D)
    weights = route_weights.reshape(-1, TOPK, 1).astype(jnp.float32)

    def forward_tiles(tiles, gate_matrix, up_matrix, down_matrix):
        expert_out, gate_pre, up_value = expert_forward(tiles[0], gate_matrix, up_matrix, down_matrix)
        return expert_out, expert_backward(tiles[1], gate_pre, up_value, gate_matrix, up_matrix, down_matrix)

    expert_out, route_grad = expert_pass(route_ids, [jnp.repeat(att_rows, TOPK, axis=0), jnp.repeat(cot_rows, TOPK, axis=0)], w_gate, w_up, w_down, forward_tiles)
    layer_out = (att_rows.astype(jnp.float32) + jnp.sum(expert_out.astype(jnp.float32).reshape(-1, TOPK, D) * weights, axis=1)).astype(jnp.bfloat16)
    attn_cot = (cot_rows.astype(jnp.float32) + jnp.sum(route_grad.astype(jnp.float32).reshape(-1, TOPK, D) * weights, axis=1)).astype(jnp.bfloat16).reshape(SEQS, LEN, D)

    def grads_of_sequence(sequence):
        def step(buffers, step_index):
            block_index = jnp.minimum(step_index, N_CTX - 1)
            live_flag = (step_index < N_CTX).astype(jnp.float32)
            query_rows = take_block(query, sequence, block_index)
            key_window = window_of(key, sequence, block_index)
            value_window = window_of(value, sequence, block_index)
            attn_probs = probs_of(query_rows, key_window, allowed_of(block_mask, sequence, block_index))
            probs_low = rounded(attn_probs)
            cot_block = take_block(attn_cot, sequence, block_index)
            att_block = take_block(attended, sequence, block_index)
            row_delta = jnp.einsum('qhd,qhd->hq', split_rows(cot_block), split_rows(att_block))
            prob_grad = jnp.einsum('qhd,khd->hqk', split_rows(cot_block), split_rows(value_window))
            score_grad = rounded(attn_probs * (prob_grad - row_delta[:, :, None]))
            query_grad = (jnp.einsum('hqk,khd->qhd', score_grad, split_rows(key_window)) * score_scale).reshape(TOK_DEV, D).astype(jnp.bfloat16)
            key_terms = (jnp.einsum('hqk,qhd->khd', score_grad, split_rows(query_rows)) * score_scale).reshape(WIN, TOK_DEV, D) * live_flag
            value_terms = jnp.einsum('hqk,qhd->khd', probs_low, split_rows(cot_block)).reshape(WIN, TOK_DEV, D) * live_flag
            blank = jnp.zeros((1, TOK_DEV, D), jnp.float32)
            key_buffer = jnp.concatenate([buffers[0][1:], blank], axis=0) + key_terms[::-1]
            value_buffer = jnp.concatenate([buffers[1][1:], blank], axis=0) + value_terms[::-1]
            return (key_buffer, value_buffer), (query_grad, key_buffer[0].astype(jnp.bfloat16), value_buffer[0].astype(jnp.bfloat16))

        start = (jnp.zeros((WIN, TOK_DEV, D), jnp.float32), jnp.zeros((WIN, TOK_DEV, D), jnp.float32))
        carry_end, emitted = lax.scan(step, start, jnp.arange(N_CTX + WIN - 1, dtype=jnp.int32))
        return (emitted[0][:N_CTX].reshape(LEN, D), emitted[1][WIN - 1:].reshape(LEN, D), emitted[2][WIN - 1:].reshape(LEN, D))

    grad_query, grad_key, grad_value = lax.map(grads_of_sequence, jnp.arange(SEQS, dtype=jnp.int32))

    def tangent_block(block):
        sequence = block // N_CTX
        block_index = block % N_CTX
        query_rows = take_block(query, sequence, block_index)
        key_window = window_of(key, sequence, block_index)
        value_window = window_of(value, sequence, block_index)
        attn_probs = probs_of(query_rows, key_window, allowed_of(block_mask, sequence, block_index))
        probs_low = rounded(attn_probs)
        tan_query = take_block(grad_query, sequence, block_index)
        tan_keys = window_of(grad_key, sequence, block_index)
        tan_values = window_of(grad_value, sequence, block_index)
        score_tan = (jnp.einsum('qhd,khd->hqk', split_rows(tan_query), split_rows(key_window)) + jnp.einsum('qhd,khd->hqk', split_rows(query_rows), split_rows(tan_keys))) * score_scale
        mean_tan = jnp.sum(attn_probs * score_tan, axis=-1, keepdims=True)
        prob_tan = rounded(attn_probs * (score_tan - mean_tan))
        out_rows = jnp.einsum('hqk,khd->qhd', prob_tan, split_rows(value_window)) + jnp.einsum('hqk,khd->qhd', probs_low, split_rows(tan_values))
        return out_rows.reshape(TOK_DEV, D).astype(jnp.bfloat16)

    attn_tangent = lax.map(tangent_block, blocks).reshape(-1, D)

    def tangent_tiles(tiles, gate_matrix, up_matrix, down_matrix):
        gate_pre = jnp.dot(tiles[0], gate_matrix, preferred_element_type=jnp.float32)
        up_value = jnp.dot(tiles[0], up_matrix, preferred_element_type=jnp.float32)
        return (expert_tangent(tiles[1], gate_pre, up_value, gate_matrix, up_matrix, down_matrix),)

    expert_tan = expert_pass(route_ids, [jnp.repeat(att_rows, TOPK, axis=0), jnp.repeat(attn_tangent, TOPK, axis=0)], w_gate, w_up, w_down, tangent_tiles)[0]
    tangent_out = (attn_tangent.astype(jnp.float32) + jnp.sum(expert_tan.astype(jnp.float32).reshape(-1, TOPK, D) * weights, axis=1)).astype(jnp.bfloat16)
    return (layer_out.reshape(SEQS, LEN, D), grad_query, grad_key, grad_value, tangent_out.reshape(SEQS, LEN, D))
```

```python
import functools

import jax
import jax.numpy as jnp
from jax import lax
from jax.experimental import pallas as pl
from jax.experimental.pallas import tpu as pltpu
from jax.sharding import PartitionSpec as P

HEADS = 16
WIN = 4
CHUNKS = 4
MESH = pl.DeviceIdType.MESH
BF16 = jnp.bfloat16
F32 = jnp.float32
HIDE = -1e30


def nn(a, b):
    return lax.dot_general(a, b, (((1,), (0,)), ((), ())), preferred_element_type=F32)


def nt(a, b):
    return lax.dot_general(a, b, (((1,), (1,)), ((), ())), preferred_element_type=F32)


def kernel(
    n_ctx, n_exp,
    q_in, k_in, v_in, c_in, ids_in, rw_in, mask_in, wg_in, wu_in, wd_in,
    lo_out, gq_out, gk_out, gv_out, to_out,
    kvw, qw, cw, gw, lsw, dlw, probs, bias, bias_t, att, cot, gqs, tan, los, tos, gqo,
    wg, wu, wd, pick, place,
    sends, recvs, gate, up, hgrad, slope_up, act,
    load_kv, load_q, load_c, load_w, put,
    ring_send, kv_recv, q_recv, c_recv, g_recv, ls_send, ls_recv, dl_send, dl_recv,
    a2a_send, a2a_recv,
):
    chunks, per = kvw.shape[1], kvw.shape[3]
    rows, width = kvw.shape[4], kvw.shape[5]
    cols = per * width
    cap = sends.shape[3]
    scale = width ** -0.5
    me = lax.axis_index("ctx")
    expert = lax.axis_index("exp")

    def span(h):
        return slice(h * width, (h + 1) * width)

    def wide(c):
        return slice(c * cols, (c + 1) * cols)

    def kv_loads(c):
        out = []
        for j in range(per):
            out.append(pltpu.make_async_copy(k_in.at[0, :, span(c * per + j)], kvw.at[0, c, 0, j], load_kv.at[c]))
            out.append(pltpu.make_async_copy(v_in.at[0, :, span(c * per + j)], kvw.at[0, c, 1, j], load_kv.at[c]))
        return out

    def q_loads(c):
        return [pltpu.make_async_copy(q_in.at[0, :, span(c * per + j)], qw.at[0, c, j], load_q.at[c]) for j in range(per)]

    c_loads = [pltpu.make_async_copy(c_in.at[0, :, wide(c)], cot.at[c], load_c.at[c]) for c in range(chunks)]
    w_loads = [
        pltpu.make_async_copy(wd_in.at[0], wd, load_w.at[0]),
        pltpu.make_async_copy(wg_in.at[0], wg, load_w.at[1]),
        pltpu.make_async_copy(wu_in.at[0], wu, load_w.at[2]),
    ]
    for c in range(chunks):
        for copy in kv_loads(c) + q_loads(c):
            copy.start()
        c_loads[c].start()
    for copy in w_loads:
        copy.start()

    barrier = pltpu.get_barrier_semaphore()
    ctx_peers = [lax.rem(me + by + n_ctx, n_ctx) for by in (1, 2, 3, -1, -2, -3)]
    exp_peers = [lax.rem(expert + r, n_exp) for r in range(n_exp)]
    exp_back = [lax.rem(expert - r + n_exp, n_exp) for r in range(n_exp)]
    for peer in ctx_peers:
        pl.semaphore_signal(barrier, inc=1, device_id={"ctx": peer}, device_id_type=MESH)
    for peer in exp_peers[1:]:
        pl.semaphore_signal(barrier, inc=1, device_id={"exp": peer}, device_id_type=MESH)

    lane = lax.broadcasted_iota(jnp.int32, (rows, 128), 1)
    ids = ids_in[0]
    hot = (lane == ids).astype(F32)
    earlier = (
        lax.broadcasted_iota(jnp.int32, (rows, rows), 0) > lax.broadcasted_iota(jnp.int32, (rows, rows), 1)
    ).astype(BF16)
    rank = jnp.sum(nn(earlier, hot.astype(BF16)) * hot, axis=1, keepdims=True)
    ahead = ids - expert
    ahead = jnp.where(ahead < 0, ahead + n_exp, ahead)
    slot = ahead.astype(F32) * cap + rank
    slots = n_exp * cap
    slot_lane = lax.broadcasted_iota(jnp.int32, (rows, slots), 1).astype(F32)
    place_f = (slot_lane == slot).astype(F32)
    place[...] = place_f.astype(BF16)
    pick[...] = place_f.T.astype(BF16)
    route_w = rw_in[0]

    qpos = lax.broadcasted_iota(jnp.int32, (rows, rows), 0)
    kpos = lax.broadcasted_iota(jnp.int32, (rows, rows), 1)
    bias[:, 0:rows] = jnp.where(qpos >= kpos, 0.0, HIDE)
    bias_t[...] = jnp.where(kpos >= qpos, 0.0, HIDE)
    hidden_by = []
    for w in range(1, WIN):
        seen = mask_in[0, :, w - 1 : w] * jnp.where(me >= w, 1, 0)
        cut = jnp.where(seen == 1, 0.0, HIDE)
        hidden_by.append(cut)
        bias[:, w * rows : (w + 1) * rows] = jnp.broadcast_to(cut, (rows, rows))

    pl.semaphore_wait(barrier, len(ctx_peers) + n_exp - 1)

    def hop(buf, send_sem, recv_sem, peer, w, c):
        return pltpu.make_async_remote_copy(
            src_ref=buf.at[w - 1, c], dst_ref=buf.at[w, c],
            send_sem=send_sem, recv_sem=recv_sem.at[w - 1, c],
            device_id={"ctx": peer}, device_id_type=MESH,
        )

    nxt, prv = ctx_peers[0], ctx_peers[3]
    kv_hop = functools.partial(hop, kvw, ring_send.at[0], kv_recv, nxt)
    q_hop = functools.partial(hop, qw, ring_send.at[1], q_recv, prv)
    c_hop = functools.partial(hop, cw, ring_send.at[2], c_recv, prv)
    g_hop = functools.partial(hop, gw, ring_send.at[3], g_recv, nxt)

    def exchange(kind, c, forward):
        peers = exp_peers if forward else exp_back
        return [
            pltpu.make_async_remote_copy(
                src_ref=sends.at[kind, r, c], dst_ref=recvs.at[kind, r, c],
                send_sem=a2a_send.at[kind], recv_sem=a2a_recv.at[kind, c],
                device_id={"exp": peers[r]}, device_id_type=MESH,
            )
            for r in range(1, n_exp)
        ]

    def send_out(kind, c, value, forward):
        parts = value.astype(BF16).reshape(n_exp, cap, cols)
        sends[kind, :, c] = parts
        recvs[kind, 0, c] = parts[0]
        for copy in exchange(kind, c, forward):
            copy.start()

    def arrived(kind, c):
        pltpu.make_async_copy(
            sends.at[kind, 1:n_exp, c], recvs.at[kind, 1:n_exp, c], a2a_recv.at[kind, c]
        ).wait()
        return recvs[kind, :, c].reshape(slots, cols)

    A, C, O, G, T, E = range(6)

    def kv_ready(c):
        pltpu.make_async_copy(kvw.at[0, c], kvw.at[0, c], load_kv.at[c]).wait()

    def q_ready(c):
        pltpu.make_async_copy(qw.at[0, c], qw.at[0, c], load_q.at[c]).wait()

    for c in range(min(2, chunks)):
        kv_ready(c)
        kv_hop(1, c).start()
        q_ready(c)
        q_hop(1, c).start()
    for c in range(chunks):
        c_loads[c].wait()
        send_out(C, c, nn(pick[...], cot[c]), True)

    lane_w = lax.broadcasted_iota(jnp.int32, (rows, 128), 1)
    lse_cols = jnp.zeros((rows, 128), F32)

    def attend(c, lse_cols):
        for j in range(per):
            h = c * per + j
            keys = jnp.concatenate([kvw[w, c, 0, j] for w in range(WIN)], axis=0)
            vals = jnp.concatenate([kvw[w, c, 1, j] for w in range(WIN)], axis=0)
            s = nt(qw[0, c, j], keys) * scale + bias[...]
            top = jnp.max(s, axis=1, keepdims=True)
            e = jnp.exp(s - top)
            total = jnp.sum(e, axis=1, keepdims=True)
            p = e * (1.0 / total)
            probs[h] = p
            lse_cols = jnp.where(lane_w == h, top + jnp.log(total), lse_cols)
            att[c, :, span(j)] = nn(p.astype(BF16), vals).astype(BF16)
        return lse_cols

    def wrows(ref, c):
        return ref[wide(c), :]

    def add_to(ref, c, value):
        if c == 0:
            ref[...] = value
        else:
            ref[...] += value

    def expert_in(c):
        x = arrived(A, c)
        add_to(gate, c, nn(x, wrows(wg, c)))
        add_to(up, c, nn(x, wrows(wu, c)))

    def expert_cot(c):
        add_to(hgrad, c, nt(arrived(C, c), wd[:, wide(c)]))

    for t in range(chunks + 3):
        if t < chunks:
            kv_hop(1, t).wait_recv()
            kv_hop(2, t).start()
            q_hop(1, t).wait_recv()
            q_hop(2, t).start()
            if t + 2 < chunks:
                kv_ready(t + 2)
                kv_hop(1, t + 2).start()
                q_ready(t + 2)
                q_hop(1, t + 2).start()
        if 0 <= t - 1 < chunks:
            kv_hop(2, t - 1).wait_recv()
            kv_hop(3, t - 1).start()
            q_hop(2, t - 1).wait_recv()
            q_hop(3, t - 1).start()
        if t == 1:
            w_loads[0].wait()
            w_loads[1].wait()
            w_loads[2].wait()
        if 0 <= t - 1 < chunks:
            expert_cot(t - 1)
        if 0 <= t - 2 < chunks:
            c = t - 2
            kv_hop(3, c).wait_recv()
            lse_cols = attend(c, lse_cols)
            send_out(A, c, nn(pick[...], att[c]), True)
        if 0 <= t - 3 < chunks:
            expert_in(t - 3)

    lse_t = lse_cols.T[0:HEADS]
    lsw[0] = lse_t
    stat_to = [None, ctx_peers[3], ctx_peers[4], ctx_peers[5]]

    def ls_copy(w):
        return pltpu.make_async_remote_copy(
            src_ref=lsw.at[WIN - 1 + w], dst_ref=lsw.at[w],
            send_sem=ls_send.at[w - 1], recv_sem=ls_recv.at[w - 1],
            device_id={"ctx": stat_to[w]}, device_id_type=MESH,
        )

    for w in range(1, WIN):
        lsw[WIN - 1 + w] = lse_t - hidden_by[w - 1]
        ls_copy(w).start()

    g, u, hg = gate[...], up[...], hgrad[...]
    sig = 1.0 / (1.0 + jnp.exp(-g))
    a = g * sig
    su = sig * (1.0 + g * (1.0 - sig)) * u
    act[...] = a
    slope_up[...] = su
    hidden = (a * u).astype(BF16)
    gate_grad = (hg * su).astype(BF16)
    up_grad = (hg * a).astype(BF16)
    for c in range(chunks):
        send_out(G, c, nt(gate_grad, wrows(wg, c)) + nt(up_grad, wrows(wu, c)), False)
    for c in range(chunks):
        send_out(O, c, nn(hidden, wd[:, wide(c)]), False)

    def dl_copy(w, c):
        return pltpu.make_async_remote_copy(
            src_ref=dlw.at[0, c], dst_ref=dlw.at[w, c],
            send_sem=dl_send.at[w - 1, c], recv_sem=dl_recv.at[w - 1, c],
            device_id={"ctx": stat_to[w]}, device_id_type=MESH,
        )

    def cot_back(c):
        x = nn(place[...], arrived(G, c)) * route_w + cot[c].astype(F32)
        new = x.astype(BF16)
        deltas = []
        cols_of = jnp.zeros((rows, 128), F32)
        for j in range(per):
            mine = new[:, span(j)]
            cw[0, c, j] = mine
            d = jnp.sum(mine.astype(F32) * att[c, :, span(j)].astype(F32), axis=1, keepdims=True)
            deltas.append(d)
            cols_of = jnp.where(lane_w == j, d, cols_of)
        dlw[0, c] = cols_of.T[0:8]
        c_hop(1, c).start()
        for w in range(1, WIN):
            dl_copy(w, c).start()
        for j in range(per):
            h = c * per + j
            keys = jnp.concatenate([kvw[w, c, 0, j] for w in range(WIN)], axis=0)
            vals = jnp.concatenate([kvw[w, c, 1, j] for w in range(WIN)], axis=0)
            ds = (probs[h] * (nt(cw[0, c, j], vals) - deltas[j])).astype(BF16)
            gq = (nn(ds, keys) * scale).astype(BF16)
            gqs[c, :, span(j)] = gq
        pltpu.make_async_copy(gqs.at[c], gq_out.at[0, :, wide(c)], put.at[0]).start()

    def key_side(c):
        for w in range(1, WIN):
            dl_copy(w, c).wait_recv()
        for j in range(per):
            h = c * per + j
            k, v = kvw[0, c, 0, j], kvw[0, c, 1, j]
            qs = jnp.concatenate([qw[w, c, j] for w in range(WIN)], axis=0)
            cs = jnp.concatenate([cw[w, c, j] for w in range(WIN)], axis=0)
            lse = jnp.concatenate([lsw[w, h : h + 1, :] for w in range(WIN)], axis=1)
            dl = jnp.concatenate([dlw[w, c, j : j + 1, :] for w in range(WIN)], axis=1)
            s = nt(k, qs) * scale - lse
            s = jnp.concatenate([s[:, 0:rows] + bias_t[...], s[:, rows:]], axis=1)
            p = jnp.exp(s)
            ds = (p * (nt(v, cs) - dl)).astype(BF16)
            gw[0, c, 0, j] = (nn(ds, qs) * scale).astype(BF16)
            gw[0, c, 1, j] = nn(p.astype(BF16), cs).astype(BF16)
        g_hop(1, c).start()
        for j in range(per):
            h = c * per + j
            pltpu.make_async_copy(gw.at[0, c, 0, j], gk_out.at[0, :, span(h)], put.at[1]).start()
            pltpu.make_async_copy(gw.at[0, c, 1, j], gv_out.at[0, :, span(h)], put.at[2]).start()

    def tangent(c):
        for j in range(per):
            h = c * per + j
            keys = jnp.concatenate([kvw[w, c, 0, j] for w in range(WIN)], axis=0)
            vals = jnp.concatenate([kvw[w, c, 1, j] for w in range(WIN)], axis=0)
            gkeys = jnp.concatenate([gw[w, c, 0, j] for w in range(WIN)], axis=0)
            gvals = jnp.concatenate([gw[w, c, 1, j] for w in range(WIN)], axis=0)
            st = (nt(gqs[c, :, span(j)], keys) + nt(qw[0, c, j], gkeys)) * scale
            p = probs[h]
            mean = jnp.sum(p * st, axis=1, keepdims=True)
            pt = (p * (st - mean)).astype(BF16)
            tan[c, :, span(j)] = (nn(pt, vals) + nn(p.astype(BF16), gvals)).astype(BF16)
        send_out(T, c, nn(pick[...], tan[c]), True)

    def layer(c):
        x = nn(place[...], arrived(O, c)) * route_w + att[c].astype(F32)
        los[c] = x.astype(BF16)
        pltpu.make_async_copy(los.at[c], lo_out.at[0, :, wide(c)], put.at[3]).start()

    def expert_tan(c):
        x = arrived(T, c)
        add_to(gate, c, nn(x, wrows(wg, c)))
        add_to(up, c, nn(x, wrows(wu, c)))

    def within(c):
        return 0 <= c < chunks

    for t in range(chunks + 7):
        if within(t - 5):
            g_hop(2, t - 5).wait_recv()
            g_hop(3, t - 5).start()
        if within(t - 4):
            g_hop(1, t - 4).wait_recv()
            g_hop(2, t - 4).start()
        if within(t - 2):
            c_hop(2, t - 2).wait_recv()
            c_hop(3, t - 2).start()
        if within(t - 1):
            c_hop(1, t - 1).wait_recv()
            c_hop(2, t - 1).start()
            q_hop(3, t - 1).wait_recv()
        if within(t):
            cot_back(t)
        if t == 2:
            for w in range(1, WIN):
                ls_copy(w).wait_recv()
        if within(t - 3):
            c_hop(3, t - 3).wait_recv()
            key_side(t - 3)
        if within(t - 6):
            g_hop(3, t - 6).wait_recv()
            tangent(t - 6)
        if within(t - 4):
            layer(t - 4)
        if within(t - 7):
            expert_tan(t - 7)

    ht = (slope_up[...] * gate[...] + act[...] * up[...]).astype(BF16)
    for c in range(chunks):
        send_out(E, c, nn(ht, wd[:, wide(c)]), False)
    for c in range(chunks):
        x = nn(place[...], arrived(E, c)) * route_w + tan[c].astype(F32)
        tos[c] = x.astype(BF16)
        pltpu.make_async_copy(tos.at[c], to_out.at[0, :, wide(c)], put.at[4]).start()

    for i, buf in enumerate((kvw, qw, cw, gw)):
        pltpu.make_async_copy(buf.at[1:WIN], buf.at[1:WIN], ring_send.at[i]).wait()
    for w in range(1, WIN):
        ls_copy(w).wait_send()
        for c in range(chunks):
            dl_copy(w, c).wait_send()
    for kind in range(6):
        part = sends.at[kind, 1:n_exp]
        pltpu.make_async_copy(part, part, a2a_send.at[kind]).wait()
    pltpu.make_async_copy(gqs, gqs, put.at[0]).wait()
    pltpu.make_async_copy(gw.at[0, :, 0], gw.at[0, :, 0], put.at[1]).wait()
    pltpu.make_async_copy(gw.at[0, :, 1], gw.at[0, :, 1], put.at[2]).wait()
    pltpu.make_async_copy(los, los, put.at[3]).wait()
    pltpu.make_async_copy(tos, tos, put.at[4]).wait()


def local(n_ctx, n_exp, query, key, value, cotangent, route_ids, route_weights, block_mask, w_gate, w_up, w_down):
    rows, model = query.shape[1:]
    ffh = w_gate.shape[2]
    width = model // HEADS
    per = HEADS // CHUNKS
    cols = per * width
    cap = 2 * rows // n_exp
    slots = n_exp * cap
    hbm = pl.BlockSpec(memory_space=pl.ANY)
    vmem = pl.BlockSpec(memory_space=pltpu.VMEM)
    dma = pltpu.SemaphoreType.DMA
    scratch = [
        pltpu.VMEM((WIN, CHUNKS, 2, per, rows, width), BF16),
        pltpu.VMEM((WIN, CHUNKS, per, rows, width), BF16),
        pltpu.VMEM((WIN, CHUNKS, per, rows, width), BF16),
        pltpu.VMEM((WIN, CHUNKS, 2, per, rows, width), BF16),
        pltpu.VMEM((2 * WIN - 1, HEADS, rows), F32),
        pltpu.VMEM((WIN, CHUNKS, 8, rows), F32),
        pltpu.VMEM((HEADS, rows, WIN * rows), F32),
        pltpu.VMEM((rows, WIN * rows), F32),
        pltpu.VMEM((rows, rows), F32),
        pltpu.VMEM((CHUNKS, rows, cols), BF16),
        pltpu.VMEM((CHUNKS, rows, cols), BF16),
        pltpu.VMEM((CHUNKS, rows, cols), BF16),
        pltpu.VMEM((CHUNKS, rows, cols), BF16),
        pltpu.VMEM((CHUNKS, rows, cols), BF16),
        pltpu.VMEM((CHUNKS, rows, cols), BF16),
        pltpu.VMEM((8, 128), F32),
        pltpu.VMEM((model, ffh), BF16),
        pltpu.VMEM((model, ffh), BF16),
        pltpu.VMEM((ffh, model), BF16),
        pltpu.VMEM((slots, rows), BF16),
        pltpu.VMEM((rows, slots), BF16),
        pltpu.VMEM((6, n_exp, CHUNKS, cap, cols), BF16),
        pltpu.VMEM((6, n_exp, CHUNKS, cap, cols), BF16),
        pltpu.VMEM((slots, ffh), F32),
        pltpu.VMEM((slots, ffh), F32),
        pltpu.VMEM((slots, ffh), F32),
        pltpu.VMEM((slots, ffh), F32),
        pltpu.VMEM((slots, ffh), F32),
        dma((CHUNKS,)), dma((CHUNKS,)), dma((CHUNKS,)), dma((3,)), dma((5,)),
        dma((4,)),
        dma((WIN - 1, CHUNKS)), dma((WIN - 1, CHUNKS)), dma((WIN - 1, CHUNKS)), dma((WIN - 1, CHUNKS)),
        dma((WIN - 1,)), dma((WIN - 1,)), dma((WIN - 1, CHUNKS)), dma((WIN - 1, CHUNKS)),
        dma((6,)), dma((6, CHUNKS)),
    ]
    out = jax.ShapeDtypeStruct((1, rows, model), BF16)
    return pl.pallas_call(
        functools.partial(kernel, n_ctx, n_exp),
        out_shape=(out,) * 5,
        in_specs=[hbm] * 4 + [vmem] * 3 + [hbm] * 3,
        out_specs=(hbm,) * 5,
        scratch_shapes=scratch,
        compiler_params=pltpu.CompilerParams(
            collective_id=0, has_side_effects=True, vmem_limit_bytes=60 * 1024 * 1024
        ),
    )(query, key, value, cotangent, route_ids, route_weights, block_mask, w_gate, w_up, w_down)


def solution(mesh):
    n_ctx, n_exp = mesh.shape["ctx"], mesh.shape["exp"]
    rows = P("exp", "ctx", None)
    weights = P("exp", None, None)
    return jax.shard_map(
        functools.partial(local, n_ctx, n_exp),
        mesh=mesh,
        in_specs=(rows,) * 7 + (weights,) * 3,
        out_specs=(rows,) * 5,
        check_vma=False,
    )
```

```python
import functools

import jax
import jax.numpy as jnp
from jax import lax
from jax.experimental import pallas as pl
from jax.experimental.pallas import tpu as pltpu
from jax.sharding import PartitionSpec as P

HEADS = 16
WIN = 4
CHUNKS = 4
MESH = pl.DeviceIdType.MESH
BF16 = jnp.bfloat16
F32 = jnp.float32
HIDE = -1e30


def nn(a, b):
    return lax.dot_general(a, b, (((1,), (0,)), ((), ())), preferred_element_type=F32)


def nt(a, b):
    return lax.dot_general(a, b, (((1,), (1,)), ((), ())), preferred_element_type=F32)


def kernel(
    n_ctx, n_exp,
    q_in, k_in, v_in, c_in, ids_in, rw_in, mask_in, wg_in, wu_in, wd_in,
    lo_out, gq_out, gk_out, gv_out, to_out,
    kvw, qw, cw, gw, lsw, dlw, probs, bias, bias_t, att, cot, gqs, tan, los, tos, kvr, gwr,
    wg, wu, wd, pick, place,
    sends, recvs, gate, up, hgrad, slope_up, act,
    load_kv, load_q, load_c, load_w, put,
    ring_send, kv_recv, q_recv, c_recv, g_recv, kv_relay, g_relay, ls_send, ls_recv, dl_send, dl_recv,
    a2a_send, a2a_recv,
):
    chunks, per = kvw.shape[1], kvw.shape[3]
    rows, width = kvw.shape[4], kvw.shape[5]
    cols = per * width
    cap = sends.shape[3]
    scale = width ** -0.5
    me = lax.axis_index("ctx")
    expert = lax.axis_index("exp")

    def span(h):
        return slice(h * width, (h + 1) * width)

    def wide(c):
        return slice(c * cols, (c + 1) * cols)

    def kv_loads(c):
        out = []
        for j in range(per):
            out.append(pltpu.make_async_copy(k_in.at[0, :, span(c * per + j)], kvw.at[0, c, 0, j], load_kv.at[c]))
            out.append(pltpu.make_async_copy(v_in.at[0, :, span(c * per + j)], kvw.at[0, c, 1, j], load_kv.at[c]))
        return out

    def q_loads(c):
        return [pltpu.make_async_copy(q_in.at[0, :, span(c * per + j)], qw.at[0, c, j], load_q.at[c]) for j in range(per)]

    c_loads = [pltpu.make_async_copy(c_in.at[0, :, wide(c)], cot.at[c], load_c.at[c]) for c in range(chunks)]
    w_loads = [
        pltpu.make_async_copy(wd_in.at[0], wd, load_w.at[0]),
        pltpu.make_async_copy(wg_in.at[0], wg, load_w.at[1]),
        pltpu.make_async_copy(wu_in.at[0], wu, load_w.at[2]),
    ]
    for c in range(chunks):
        for copy in kv_loads(c) + q_loads(c):
            copy.start()
        c_loads[c].start()
    for copy in w_loads:
        copy.start()

    barrier = pltpu.get_barrier_semaphore()
    ctx_peers = [lax.rem(me + by + n_ctx, n_ctx) for by in (1, 2, 3, -1, -2, -3)]
    half, last = n_ctx // 2, n_ctx - 1
    far_peers = [lax.rem(me + by, n_ctx) for by in (half, half - 1, half + 1)]
    exp_peers = [lax.rem(expert + r, n_exp) for r in range(n_exp)]
    exp_back = [lax.rem(expert - r + n_exp, n_exp) for r in range(n_exp)]
    for peer in ctx_peers + far_peers:
        pl.semaphore_signal(barrier, inc=1, device_id={"ctx": peer}, device_id_type=MESH)
    for peer in exp_peers[1:]:
        pl.semaphore_signal(barrier, inc=1, device_id={"exp": peer}, device_id_type=MESH)

    lane = lax.broadcasted_iota(jnp.int32, (rows, 128), 1)
    eye = lax.broadcasted_iota(jnp.int32, (rows, rows), 0) == lax.broadcasted_iota(jnp.int32, (rows, rows), 1)
    ids = jnp.sum(jnp.where(eye, ids_in[0].astype(F32), 0.0), axis=1, keepdims=True).astype(jnp.int32)
    hot = (lane == ids).astype(F32)
    earlier = (
        lax.broadcasted_iota(jnp.int32, (rows, rows), 0) > lax.broadcasted_iota(jnp.int32, (rows, rows), 1)
    ).astype(BF16)
    rank = jnp.sum(nn(earlier, hot.astype(BF16)) * hot, axis=1, keepdims=True)
    ahead = ids - expert
    ahead = jnp.where(ahead < 0, ahead + n_exp, ahead)
    slot = ahead.astype(F32) * cap + rank
    slots = n_exp * cap
    slot_lane = lax.broadcasted_iota(jnp.int32, (rows, slots), 1).astype(F32)
    place_f = (slot_lane == slot).astype(F32)
    place[...] = place_f.astype(BF16)
    pick[...] = place_f.T.astype(BF16)
    route_w = jnp.sum(jnp.where(eye, rw_in[0], 0.0), axis=1, keepdims=True)

    qpos = lax.broadcasted_iota(jnp.int32, (rows, rows), 0)
    kpos = lax.broadcasted_iota(jnp.int32, (rows, rows), 1)
    bias[:, 0:rows] = jnp.where(qpos >= kpos, 0.0, HIDE)
    bias_t[...] = jnp.where(kpos >= qpos, 0.0, HIDE)
    hidden_by = []
    for w in range(1, WIN):
        seen = mask_in[0, :, w - 1 : w] * jnp.where(me >= w, 1, 0)
        cut = jnp.where(seen == 1, 0.0, HIDE)
        hidden_by.append(cut)
        bias[:, w * rows : (w + 1) * rows] = jnp.broadcast_to(cut, (rows, rows))

    pl.semaphore_wait(barrier, len(ctx_peers) + len(far_peers) + n_exp - 1)

    def hop(buf, send_sem, recv_sem, peer, w, c):
        return pltpu.make_async_remote_copy(
            src_ref=buf.at[w - 1, c], dst_ref=buf.at[w, c],
            send_sem=send_sem, recv_sem=recv_sem.at[w - 1, c],
            device_id={"ctx": peer}, device_id_type=MESH,
        )

    nxt, prv = ctx_peers[0], ctx_peers[3]

    class Forward:
        def __init__(self, buf, relay, send_sem, recv_sem, relay_sem):
            self.buf, self.relay, self.send_sem, self.recv_sem, self.relay_sem = buf, relay, send_sem, recv_sem, relay_sem

        def copy(self, src, dst, recv_sem, peer):
            return pltpu.make_async_remote_copy(
                src_ref=src, dst_ref=dst, send_sem=self.send_sem, recv_sem=recv_sem,
                device_id={"ctx": peer}, device_id_type=MESH,
            )

        def send(self, w, c):
            src, dst = self.buf.at[w - 1, c], self.buf.at[w, c]
            sem = self.recv_sem.at[w - 1, c]

            @pl.when((me < last) & (me != half - 1))
            def _():
                self.copy(src, dst, sem, nxt).start()

            @pl.when(me == half - 1)
            def _():
                self.copy(src.at[1], self.relay.at[w - 1, c], self.relay_sem.at[w - 1, c], last).start()
                self.copy(src.at[0], dst.at[0], sem, half).start()

        def wait(self, w, c):
            @pl.when(me == last)
            def _():
                part = self.relay.at[w - 1, c]
                pltpu.make_async_copy(part, part, self.relay_sem.at[w - 1, c]).wait()
                self.copy(part, self.buf.at[w, c, 1], self.recv_sem.at[w - 1, c], half).start()

            @pl.when(me > 0)
            def _():
                part = self.buf.at[w, c]
                pltpu.make_async_copy(part, part, self.recv_sem.at[w - 1, c]).wait()

        def finish(self):
            @pl.when(me < last)
            def _():
                pltpu.make_async_copy(self.buf.at[1:WIN], self.buf.at[1:WIN], self.send_sem).wait()

            @pl.when(me == last)
            def _():
                pltpu.make_async_copy(self.relay, self.relay, self.send_sem).wait()

    class Backward:
        def __init__(self, buf, send_sem, recv_sem):
            self.buf, self.send_sem, self.recv_sem = buf, send_sem, recv_sem

        def send(self, w, c):
            @pl.when(me > 0)
            def _():
                hop(self.buf, self.send_sem, self.recv_sem, prv, w, c).start()

        def wait(self, w, c):
            @pl.when(me < last)
            def _():
                hop(self.buf, self.send_sem, self.recv_sem, prv, w, c).wait_recv()

        def finish(self):
            @pl.when(me > 0)
            def _():
                pltpu.make_async_copy(self.buf.at[1:WIN], self.buf.at[1:WIN], self.send_sem).wait()

    kv = Forward(kvw, kvr, ring_send.at[0], kv_recv, kv_relay)
    gr = Forward(gw, gwr, ring_send.at[3], g_recv, g_relay)
    qb = Backward(qw, ring_send.at[1], q_recv)
    cb = Backward(cw, ring_send.at[2], c_recv)

    @pl.when(me == 0)
    def _():
        kvw[1:WIN] = jnp.zeros((WIN - 1,) + kvw.shape[1:], BF16)
        gw[1:WIN] = jnp.zeros((WIN - 1,) + gw.shape[1:], BF16)

    @pl.when(me == last)
    def _():
        qw[1:WIN] = jnp.zeros((WIN - 1,) + qw.shape[1:], BF16)
        cw[1:WIN] = jnp.zeros((WIN - 1,) + cw.shape[1:], BF16)

    def exchange(kind, c, forward):
        peers = exp_peers if forward else exp_back
        return [
            pltpu.make_async_remote_copy(
                src_ref=sends.at[kind, r, c], dst_ref=recvs.at[kind, r, c],
                send_sem=a2a_send.at[kind], recv_sem=a2a_recv.at[kind, c],
                device_id={"exp": peers[r]}, device_id_type=MESH,
            )
            for r in range(1, n_exp)
        ]

    def send_out(kind, c, value, forward):
        parts = value.astype(BF16).reshape(n_exp, cap, cols)
        sends[kind, :, c] = parts
        recvs[kind, 0, c] = parts[0]
        for copy in exchange(kind, c, forward):
            copy.start()

    def arrived(kind, c):
        pltpu.make_async_copy(
            sends.at[kind, 1:n_exp, c], recvs.at[kind, 1:n_exp, c], a2a_recv.at[kind, c]
        ).wait()
        return recvs[kind, :, c].reshape(slots, cols)

    A, C, O, G, T, E = range(6)

    def kv_ready(c):
        pltpu.make_async_copy(kvw.at[0, c], kvw.at[0, c], load_kv.at[c]).wait()

    def q_ready(c):
        pltpu.make_async_copy(qw.at[0, c], qw.at[0, c], load_q.at[c]).wait()

    for c in range(min(2, chunks)):
        kv_ready(c)
        kv.send(1, c)
        q_ready(c)
        qb.send(1, c)
    for c in range(chunks):
        c_loads[c].wait()
        send_out(C, c, nn(pick[...], cot[c]), True)

    lane_w = lax.broadcasted_iota(jnp.int32, (rows, 128), 1)
    lse_cols = jnp.zeros((rows, 128), F32)

    def attend(c, lse_cols):
        for j in range(per):
            h = c * per + j
            keys = jnp.concatenate([kvw[w, c, 0, j] for w in range(WIN)], axis=0)
            vals = jnp.concatenate([kvw[w, c, 1, j] for w in range(WIN)], axis=0)
            s = nt(qw[0, c, j], keys) * scale + bias[...]
            top = jnp.max(s, axis=1, keepdims=True)
            e = jnp.exp(s - top)
            total = jnp.sum(e, axis=1, keepdims=True)
            p = e * (1.0 / total)
            probs[h] = p
            lse_cols = jnp.where(lane_w == h, top + jnp.log(total), lse_cols)
            att[c, :, span(j)] = nn(p.astype(BF16), vals).astype(BF16)
        return lse_cols

    def wrows(ref, c):
        return ref[wide(c), :]

    def add_to(ref, c, value):
        if c == 0:
            ref[...] = value
        else:
            ref[...] += value

    def expert_in(c):
        x = arrived(A, c)
        add_to(gate, c, nn(x, wrows(wg, c)))
        add_to(up, c, nn(x, wrows(wu, c)))

    def expert_cot(c):
        add_to(hgrad, c, nt(arrived(C, c), wd[:, wide(c)]))

    for t in range(chunks + 3):
        if t + 2 < chunks:
            kv_ready(t + 2)
            kv.send(1, t + 2)
            q_ready(t + 2)
            qb.send(1, t + 2)
        if t < chunks:
            kv.wait(1, t)
            kv.send(2, t)
            qb.wait(1, t)
            qb.send(2, t)
        if 0 <= t - 1 < chunks:
            kv.wait(2, t - 1)
            kv.send(3, t - 1)
            qb.wait(2, t - 1)
            qb.send(3, t - 1)
        if t == 1:
            w_loads[0].wait()
            w_loads[1].wait()
            w_loads[2].wait()
        if 0 <= t - 1 < chunks:
            expert_cot(t - 1)
        if 0 <= t - 2 < chunks:
            c = t - 2
            kv.wait(3, c)
            lse_cols = attend(c, lse_cols)
            send_out(A, c, nn(pick[...], att[c]), True)
        if 0 <= t - 3 < chunks:
            expert_in(t - 3)

    lse_t = lse_cols.T[0:HEADS]
    lsw[0] = lse_t
    stat_to = [None, ctx_peers[3], ctx_peers[4], ctx_peers[5]]

    def ls_copy(w):
        return pltpu.make_async_remote_copy(
            src_ref=lsw.at[WIN - 1 + w], dst_ref=lsw.at[w],
            send_sem=ls_send.at[w - 1], recv_sem=ls_recv.at[w - 1],
            device_id={"ctx": stat_to[w]}, device_id_type=MESH,
        )

    for w in range(1, WIN):
        lsw[WIN - 1 + w] = lse_t - hidden_by[w - 1]
        ls_copy(w).start()

    g, u, hg = gate[...], up[...], hgrad[...]
    sig = 1.0 / (1.0 + jnp.exp(-g))
    a = g * sig
    su = sig * (1.0 + g * (1.0 - sig)) * u
    act[...] = a
    slope_up[...] = su
    hidden = (a * u).astype(BF16)
    gate_grad = (hg * su).astype(BF16)
    up_grad = (hg * a).astype(BF16)
    for c in range(chunks):
        send_out(G, c, nt(gate_grad, wrows(wg, c)) + nt(up_grad, wrows(wu, c)), False)
    for c in range(chunks):
        send_out(O, c, nn(hidden, wd[:, wide(c)]), False)

    def dl_copy(w, c):
        return pltpu.make_async_remote_copy(
            src_ref=dlw.at[0, c], dst_ref=dlw.at[w, c],
            send_sem=dl_send.at[w - 1, c], recv_sem=dl_recv.at[w - 1, c],
            device_id={"ctx": stat_to[w]}, device_id_type=MESH,
        )

    def cot_back(c):
        x = nn(place[...], arrived(G, c)) * route_w + cot[c].astype(F32)
        new = x.astype(BF16)
        deltas = []
        cols_of = jnp.zeros((rows, 128), F32)
        for j in range(per):
            mine = new[:, span(j)]
            cw[0, c, j] = mine
            d = jnp.sum(mine.astype(F32) * att[c, :, span(j)].astype(F32), axis=1, keepdims=True)
            deltas.append(d)
            cols_of = jnp.where(lane_w == j, d, cols_of)
        dlw[0, c] = cols_of.T[0:8]
        cb.send(1, c)
        for w in range(1, WIN):
            dl_copy(w, c).start()
        for j in range(per):
            h = c * per + j
            keys = jnp.concatenate([kvw[w, c, 0, j] for w in range(WIN)], axis=0)
            vals = jnp.concatenate([kvw[w, c, 1, j] for w in range(WIN)], axis=0)
            ds = (probs[h] * (nt(cw[0, c, j], vals) - deltas[j])).astype(BF16)
            gq = (nn(ds, keys) * scale).astype(BF16)
            gqs[c, :, span(j)] = gq
        pltpu.make_async_copy(gqs.at[c], gq_out.at[0, :, wide(c)], put.at[0]).start()

    def key_side(c):
        for w in range(1, WIN):
            dl_copy(w, c).wait_recv()
        for j in range(per):
            h = c * per + j
            k, v = kvw[0, c, 0, j], kvw[0, c, 1, j]
            qs = jnp.concatenate([qw[w, c, j] for w in range(WIN)], axis=0)
            cs = jnp.concatenate([cw[w, c, j] for w in range(WIN)], axis=0)
            lse = jnp.concatenate([lsw[w, h : h + 1, :] for w in range(WIN)], axis=1)
            dl = jnp.concatenate([dlw[w, c, j : j + 1, :] for w in range(WIN)], axis=1)
            s = nt(k, qs) * scale - lse
            s = jnp.concatenate([s[:, 0:rows] + bias_t[...], s[:, rows:]], axis=1)
            p = jnp.exp(s)
            ds = (p * (nt(v, cs) - dl)).astype(BF16)
            gw[0, c, 0, j] = (nn(ds, qs) * scale).astype(BF16)
            gw[0, c, 1, j] = nn(p.astype(BF16), cs).astype(BF16)
        gr.send(1, c)
        for j in range(per):
            h = c * per + j
            pltpu.make_async_copy(gw.at[0, c, 0, j], gk_out.at[0, :, span(h)], put.at[1]).start()
            pltpu.make_async_copy(gw.at[0, c, 1, j], gv_out.at[0, :, span(h)], put.at[2]).start()

    def tangent(c):
        for j in range(per):
            h = c * per + j
            keys = jnp.concatenate([kvw[w, c, 0, j] for w in range(WIN)], axis=0)
            vals = jnp.concatenate([kvw[w, c, 1, j] for w in range(WIN)], axis=0)
            gkeys = jnp.concatenate([gw[w, c, 0, j] for w in range(WIN)], axis=0)
            gvals = jnp.concatenate([gw[w, c, 1, j] for w in range(WIN)], axis=0)
            st = (nt(gqs[c, :, span(j)], keys) + nt(qw[0, c, j], gkeys)) * scale
            p = probs[h]
            mean = jnp.sum(p * st, axis=1, keepdims=True)
            pt = (p * (st - mean)).astype(BF16)
            tan[c, :, span(j)] = (nn(pt, vals) + nn(p.astype(BF16), gvals)).astype(BF16)
        send_out(T, c, nn(pick[...], tan[c]), True)

    def layer(c):
        x = nn(place[...], arrived(O, c)) * route_w + att[c].astype(F32)
        los[c] = x.astype(BF16)
        pltpu.make_async_copy(los.at[c], lo_out.at[0, :, wide(c)], put.at[3]).start()

    def expert_tan(c):
        x = arrived(T, c)
        add_to(gate, c, nn(x, wrows(wg, c)))
        add_to(up, c, nn(x, wrows(wu, c)))

    def within(c):
        return 0 <= c < chunks

    for t in range(chunks + 7):
        if within(t - 5):
            gr.wait(2, t - 5)
            gr.send(3, t - 5)
        if within(t - 4):
            gr.wait(1, t - 4)
            gr.send(2, t - 4)
        if within(t - 2):
            cb.wait(2, t - 2)
            cb.send(3, t - 2)
        if within(t - 1):
            cb.wait(1, t - 1)
            cb.send(2, t - 1)
            qb.wait(3, t - 1)
        if within(t):
            cot_back(t)
        if t == 2:
            for w in range(1, WIN):
                ls_copy(w).wait_recv()
        if within(t - 3):
            cb.wait(3, t - 3)
            key_side(t - 3)
        if within(t - 6):
            gr.wait(3, t - 6)
            tangent(t - 6)
        if within(t - 4):
            layer(t - 4)
        if within(t - 7):
            expert_tan(t - 7)

    ht = (slope_up[...] * gate[...] + act[...] * up[...]).astype(BF16)
    for c in range(chunks):
        send_out(E, c, nn(ht, wd[:, wide(c)]), False)
    for c in range(chunks):
        x = nn(place[...], arrived(E, c)) * route_w + tan[c].astype(F32)
        tos[c] = x.astype(BF16)
        pltpu.make_async_copy(tos.at[c], to_out.at[0, :, wide(c)], put.at[4]).start()

    for chain in (kv, gr, qb, cb):
        chain.finish()
    for w in range(1, WIN):
        ls_copy(w).wait_send()
        for c in range(chunks):
            dl_copy(w, c).wait_send()
    for kind in range(6):
        part = sends.at[kind, 1:n_exp]
        pltpu.make_async_copy(part, part, a2a_send.at[kind]).wait()
    pltpu.make_async_copy(gqs, gqs, put.at[0]).wait()
    pltpu.make_async_copy(gw.at[0, :, 0], gw.at[0, :, 0], put.at[1]).wait()
    pltpu.make_async_copy(gw.at[0, :, 1], gw.at[0, :, 1], put.at[2]).wait()
    pltpu.make_async_copy(los, los, put.at[3]).wait()
    pltpu.make_async_copy(tos, tos, put.at[4]).wait()


def hand_over(*refs):
    ins, outs, sems = refs[:5], refs[5:10], refs[10]
    copies = [pltpu.make_async_copy(a, b, sems.at[i]) for i, (a, b) in enumerate(zip(ins, outs))]
    for copy in copies:
        copy.start()
    for copy in copies:
        copy.wait()


def local(n_ctx, n_exp, query, key, value, cotangent, route_ids, route_weights, block_mask, w_gate, w_up, w_down):
    rows, model = query.shape[1:]
    ffh = w_gate.shape[2]
    width = model // HEADS
    per = HEADS // CHUNKS
    cols = per * width
    cap = 2 * rows // n_exp
    slots = n_exp * cap
    hbm = pl.BlockSpec(memory_space=pl.ANY)
    vmem = pl.BlockSpec(memory_space=pltpu.VMEM)
    dma = pltpu.SemaphoreType.DMA
    scratch = [
        pltpu.VMEM((WIN, CHUNKS, 2, per, rows, width), BF16),
        pltpu.VMEM((WIN, CHUNKS, per, rows, width), BF16),
        pltpu.VMEM((WIN, CHUNKS, per, rows, width), BF16),
        pltpu.VMEM((WIN, CHUNKS, 2, per, rows, width), BF16),
        pltpu.VMEM((2 * WIN - 1, HEADS, rows), F32),
        pltpu.VMEM((WIN, CHUNKS, 8, rows), F32),
        pltpu.VMEM((HEADS, rows, WIN * rows), F32),
        pltpu.VMEM((rows, WIN * rows), F32),
        pltpu.VMEM((rows, rows), F32),
        pltpu.VMEM((CHUNKS, rows, cols), BF16),
        pltpu.VMEM((CHUNKS, rows, cols), BF16),
        pltpu.VMEM((CHUNKS, rows, cols), BF16),
        pltpu.VMEM((CHUNKS, rows, cols), BF16),
        pltpu.VMEM((CHUNKS, rows, cols), BF16),
        pltpu.VMEM((CHUNKS, rows, cols), BF16),
        pltpu.VMEM((WIN - 1, CHUNKS, per, rows, width), BF16),
        pltpu.VMEM((WIN - 1, CHUNKS, per, rows, width), BF16),
        pltpu.VMEM((model, ffh), BF16),
        pltpu.VMEM((model, ffh), BF16),
        pltpu.VMEM((ffh, model), BF16),
        pltpu.VMEM((slots, rows), BF16),
        pltpu.VMEM((rows, slots), BF16),
        pltpu.VMEM((6, n_exp, CHUNKS, cap, cols), BF16),
        pltpu.VMEM((6, n_exp, CHUNKS, cap, cols), BF16),
        pltpu.VMEM((slots, ffh), F32),
        pltpu.VMEM((slots, ffh), F32),
        pltpu.VMEM((slots, ffh), F32),
        pltpu.VMEM((slots, ffh), F32),
        pltpu.VMEM((slots, ffh), F32),
        dma((CHUNKS,)), dma((CHUNKS,)), dma((CHUNKS,)), dma((3,)), dma((5,)),
        dma((4,)),
        dma((WIN - 1, CHUNKS)), dma((WIN - 1, CHUNKS)), dma((WIN - 1, CHUNKS)), dma((WIN - 1, CHUNKS)),
        dma((WIN - 1, CHUNKS)), dma((WIN - 1, CHUNKS)),
        dma((WIN - 1,)), dma((WIN - 1,)), dma((WIN - 1, CHUNKS)), dma((WIN - 1, CHUNKS)),
        dma((6,)), dma((6, CHUNKS)),
    ]
    out = jax.ShapeDtypeStruct((1, rows, model), BF16)
    results = pl.pallas_call(
        functools.partial(kernel, n_ctx, n_exp),
        out_shape=(out,) * 5,
        in_specs=[hbm] * 4 + [vmem] * 3 + [hbm] * 3,
        out_specs=(hbm,) * 5,
        scratch_shapes=scratch,
        compiler_params=pltpu.CompilerParams(
            collective_id=0, has_side_effects=True, vmem_limit_bytes=60 * 1024 * 1024
        ),
    )(
        query, key, value, cotangent, route_ids.reshape(1, 1, rows), route_weights.reshape(1, 1, rows),
        block_mask, w_gate, w_up, w_down,
    )
    return pl.pallas_call(
        hand_over,
        out_shape=(out,) * 5,
        in_specs=[hbm] * 5,
        out_specs=(hbm,) * 5,
        scratch_shapes=[dma((5,))],
    )(*results)


def solution(mesh):
    n_ctx, n_exp = mesh.shape["ctx"], mesh.shape["exp"]
    rows = P("exp", "ctx", None)
    weights = P("exp", None, None)
    return jax.shard_map(
        functools.partial(local, n_ctx, n_exp),
        mesh=mesh,
        in_specs=(rows,) * 7 + (weights,) * 3,
        out_specs=(rows,) * 5,
        check_vma=False,
    )
```

```python
import functools

import jax
import jax.numpy as jnp
from jax import lax
from jax.experimental import pallas as pl
from jax.experimental.pallas import tpu as pltpu
from jax.sharding import PartitionSpec as P

HEADS = 16
WIN = 4
CHUNKS = 4
MESH = pl.DeviceIdType.MESH
BF16 = jnp.bfloat16
F32 = jnp.float32
HIDE = -1e30


def nn(a, b):
    return lax.dot_general(a, b, (((1,), (0,)), ((), ())), preferred_element_type=F32)


def tn(a, b):
    return lax.dot_general(a, b, (((0,), (0,)), ((), ())), preferred_element_type=F32)


def nt(a, b):
    return lax.dot_general(a, b, (((1,), (1,)), ((), ())), preferred_element_type=F32)


def kernel(
    n_ctx, n_exp,
    q_in, k_in, v_in, c_in, ids_in, rw_in, mask_in, wg_in, wu_in, wd_in,
    lo_out, gq_out, gk_out, gv_out, to_out,
    kvw, qw, cw, gkv, us, ur, uloc, t1, m2s, m2r, lsw, dlw, probs, bias, bias_t, att, cot, gqs, tan, los, tos, kvr,
    wg, wu, wd, pick, place,
    sends, recvs, gate, up, hgrad, slope_up, act,
    load_kv, load_q, load_c, load_w, put,
    ring_send, kv_recv, q_recv, c_recv, u_recv, kv_relay, m2_send, m2_recv, ls_send, ls_recv, dl_send, dl_recv,
    a2a_send, a2a_recv,
):
    chunks, per = kvw.shape[1], kvw.shape[3]
    rows, width = kvw.shape[4], kvw.shape[5]
    cols = per * width
    cap = sends.shape[3]
    scale = width ** -0.5
    me = lax.axis_index("ctx")
    expert = lax.axis_index("exp")

    def span(h):
        return slice(h * width, (h + 1) * width)

    def wide(c):
        return slice(c * cols, (c + 1) * cols)

    def kv_loads(c):
        out = []
        for j in range(per):
            out.append(pltpu.make_async_copy(k_in.at[0, :, span(c * per + j)], kvw.at[0, c, 0, j], load_kv.at[c]))
            out.append(pltpu.make_async_copy(v_in.at[0, :, span(c * per + j)], kvw.at[0, c, 1, j], load_kv.at[c]))
        return out

    def q_loads(c):
        return [pltpu.make_async_copy(q_in.at[0, :, span(c * per + j)], qw.at[0, c, j], load_q.at[c]) for j in range(per)]

    c_loads = [pltpu.make_async_copy(c_in.at[0, :, wide(c)], cot.at[c], load_c.at[c]) for c in range(chunks)]
    w_loads = [
        pltpu.make_async_copy(wd_in.at[0], wd, load_w.at[0]),
        pltpu.make_async_copy(wg_in.at[0], wg, load_w.at[1]),
        pltpu.make_async_copy(wu_in.at[0], wu, load_w.at[2]),
    ]
    for c in range(chunks):
        for copy in kv_loads(c) + q_loads(c):
            copy.start()
        c_loads[c].start()
    for copy in w_loads:
        copy.start()

    barrier = pltpu.get_barrier_semaphore()
    ctx_peers = [lax.rem(me + by + n_ctx, n_ctx) for by in (1, 2, 3, -1, -2, -3)]
    half, last = n_ctx // 2, n_ctx - 1
    far_peers = [lax.rem(me + by, n_ctx) for by in (half, half - 1, half + 1)]
    exp_peers = [lax.rem(expert + r, n_exp) for r in range(n_exp)]
    exp_back = [lax.rem(expert - r + n_exp, n_exp) for r in range(n_exp)]
    for peer in ctx_peers + far_peers:
        pl.semaphore_signal(barrier, inc=1, device_id={"ctx": peer}, device_id_type=MESH)
    for peer in exp_peers[1:]:
        pl.semaphore_signal(barrier, inc=1, device_id={"exp": peer}, device_id_type=MESH)

    lane = lax.broadcasted_iota(jnp.int32, (rows, 128), 1)
    eye = lax.broadcasted_iota(jnp.int32, (rows, rows), 0) == lax.broadcasted_iota(jnp.int32, (rows, rows), 1)
    ids = jnp.sum(jnp.where(eye, ids_in[0].astype(F32), 0.0), axis=1, keepdims=True).astype(jnp.int32)
    hot = (lane == ids).astype(F32)
    earlier = (
        lax.broadcasted_iota(jnp.int32, (rows, rows), 0) > lax.broadcasted_iota(jnp.int32, (rows, rows), 1)
    ).astype(BF16)
    rank = jnp.sum(nn(earlier, hot.astype(BF16)) * hot, axis=1, keepdims=True)
    ahead = ids - expert
    ahead = jnp.where(ahead < 0, ahead + n_exp, ahead)
    slot = ahead.astype(F32) * cap + rank
    slots = n_exp * cap
    slot_lane = lax.broadcasted_iota(jnp.int32, (rows, slots), 1).astype(F32)
    place_f = (slot_lane == slot).astype(F32)
    place[...] = place_f.astype(BF16)
    pick[...] = place_f.T.astype(BF16)
    route_w = jnp.sum(jnp.where(eye, rw_in[0], 0.0), axis=1, keepdims=True)

    qpos = lax.broadcasted_iota(jnp.int32, (rows, rows), 0)
    kpos = lax.broadcasted_iota(jnp.int32, (rows, rows), 1)
    bias[:, 0:rows] = jnp.where(qpos >= kpos, 0.0, HIDE)
    bias_t[...] = jnp.where(kpos >= qpos, 0.0, HIDE)
    hidden_by = []
    for w in range(1, WIN):
        seen = mask_in[0, :, w - 1 : w] * jnp.where(me >= w, 1, 0)
        cut = jnp.where(seen == 1, 0.0, HIDE)
        hidden_by.append(cut)
        bias[:, w * rows : (w + 1) * rows] = jnp.broadcast_to(cut, (rows, rows))

    pl.semaphore_wait(barrier, len(ctx_peers) + len(far_peers) + n_exp - 1)

    def hop(buf, send_sem, recv_sem, peer, w, c):
        return pltpu.make_async_remote_copy(
            src_ref=buf.at[w - 1, c], dst_ref=buf.at[w, c],
            send_sem=send_sem, recv_sem=recv_sem.at[w - 1, c],
            device_id={"ctx": peer}, device_id_type=MESH,
        )

    nxt, prv = ctx_peers[0], ctx_peers[3]

    class Forward:
        def __init__(self, buf, relay, send_sem, recv_sem, relay_sem):
            self.buf, self.relay, self.send_sem, self.recv_sem, self.relay_sem = buf, relay, send_sem, recv_sem, relay_sem

        def copy(self, src, dst, recv_sem, peer):
            return pltpu.make_async_remote_copy(
                src_ref=src, dst_ref=dst, send_sem=self.send_sem, recv_sem=recv_sem,
                device_id={"ctx": peer}, device_id_type=MESH,
            )

        def send(self, w, c):
            src, dst = self.buf.at[w - 1, c], self.buf.at[w, c]
            sem = self.recv_sem.at[w - 1, c]

            @pl.when((me < last) & (me != half - 1))
            def _():
                self.copy(src, dst, sem, nxt).start()

            @pl.when(me == half - 1)
            def _():
                self.copy(src.at[1], self.relay.at[w - 1, c], self.relay_sem.at[w - 1, c], last).start()
                self.copy(src.at[0], dst.at[0], sem, half).start()

        def wait(self, w, c):
            @pl.when(me == last)
            def _():
                part = self.relay.at[w - 1, c]
                pltpu.make_async_copy(part, part, self.relay_sem.at[w - 1, c]).wait()
                self.copy(part, self.buf.at[w, c, 1], self.recv_sem.at[w - 1, c], half).start()

            @pl.when(me > 0)
            def _():
                part = self.buf.at[w, c]
                pltpu.make_async_copy(part, part, self.recv_sem.at[w - 1, c]).wait()

        def finish(self):
            @pl.when(me < last)
            def _():
                pltpu.make_async_copy(self.buf.at[1:WIN], self.buf.at[1:WIN], self.send_sem).wait()

            @pl.when(me == last)
            def _():
                pltpu.make_async_copy(self.relay, self.relay, self.send_sem).wait()

    class Backward:
        def __init__(self, buf, send_sem, recv_sem):
            self.buf, self.send_sem, self.recv_sem = buf, send_sem, recv_sem

        def send(self, w, c):
            @pl.when(me > 0)
            def _():
                hop(self.buf, self.send_sem, self.recv_sem, prv, w, c).start()

        def wait(self, w, c):
            @pl.when(me < last)
            def _():
                hop(self.buf, self.send_sem, self.recv_sem, prv, w, c).wait_recv()

        def finish(self):
            @pl.when(me > 0)
            def _():
                pltpu.make_async_copy(self.buf.at[1:WIN], self.buf.at[1:WIN], self.send_sem).wait()

    kv = Forward(kvw, kvr, ring_send.at[0], kv_recv, kv_relay)

    class Sums:
        def copy(self, w, c):
            return pltpu.make_async_remote_copy(
                src_ref=us.at[w - 1, c], dst_ref=ur.at[w - 1, c], send_sem=ring_send.at[3], recv_sem=u_recv.at[w - 1, c],
                device_id={"ctx": nxt}, device_id_type=MESH,
            )

        def send(self, w, c):
            @pl.when(me < last)
            def _():
                self.copy(w, c).start()

        def wait(self, w, c):
            @pl.when(me > 0)
            def _():
                self.copy(w, c).wait_recv()

        def finish(self):
            @pl.when(me < last)
            def _():
                pltpu.make_async_copy(us, us, ring_send.at[3]).wait()

    su_chain = Sums()
    qb = Backward(qw, ring_send.at[1], q_recv)
    cb = Backward(cw, ring_send.at[2], c_recv)

    m2s[...] = jnp.zeros(m2s.shape, F32)

    @pl.when(me == 0)
    def _():
        kvw[1:WIN] = jnp.zeros((WIN - 1,) + kvw.shape[1:], BF16)
        ur[...] = jnp.zeros(ur.shape, BF16)

    @pl.when(me == last)
    def _():
        qw[1:WIN] = jnp.zeros((WIN - 1,) + qw.shape[1:], BF16)
        cw[1:WIN] = jnp.zeros((WIN - 1,) + cw.shape[1:], BF16)

    def exchange(kind, c, forward):
        peers = exp_peers if forward else exp_back
        return [
            pltpu.make_async_remote_copy(
                src_ref=sends.at[kind, r, c], dst_ref=recvs.at[kind, r, c],
                send_sem=a2a_send.at[kind], recv_sem=a2a_recv.at[kind, c],
                device_id={"exp": peers[r]}, device_id_type=MESH,
            )
            for r in range(1, n_exp)
        ]

    def send_out(kind, c, value, forward):
        parts = value.astype(BF16).reshape(n_exp, cap, cols)
        sends[kind, :, c] = parts
        recvs[kind, 0, c] = parts[0]
        for copy in exchange(kind, c, forward):
            copy.start()

    def arrived(kind, c):
        pltpu.make_async_copy(
            sends.at[kind, 1:n_exp, c], recvs.at[kind, 1:n_exp, c], a2a_recv.at[kind, c]
        ).wait()
        return recvs[kind, :, c].reshape(slots, cols)

    A, C, O, G, T, E = range(6)

    def kv_ready(c):
        pltpu.make_async_copy(kvw.at[0, c], kvw.at[0, c], load_kv.at[c]).wait()

    def q_ready(c):
        pltpu.make_async_copy(qw.at[0, c], qw.at[0, c], load_q.at[c]).wait()

    for c in range(min(2, chunks)):
        kv_ready(c)
        kv.send(1, c)
        q_ready(c)
        qb.send(1, c)
    for c in range(chunks):
        c_loads[c].wait()
        send_out(C, c, nn(pick[...], cot[c]), True)

    lane_w = lax.broadcasted_iota(jnp.int32, (rows, 128), 1)
    lse_cols = jnp.zeros((rows, 128), F32)

    def attend(c, lse_cols):
        for j in range(per):
            h = c * per + j
            keys = jnp.concatenate([kvw[w, c, 0, j] for w in range(WIN)], axis=0)
            vals = jnp.concatenate([kvw[w, c, 1, j] for w in range(WIN)], axis=0)
            s = nt(qw[0, c, j], keys) * scale + bias[...]
            top = jnp.max(s, axis=1, keepdims=True)
            e = jnp.exp(s - top)
            total = jnp.sum(e, axis=1, keepdims=True)
            p = e * (1.0 / total)
            probs[h] = p
            lse_cols = jnp.where(lane_w == h, top + jnp.log(total), lse_cols)
            att[c, :, span(j)] = nn(p.astype(BF16), vals).astype(BF16)
        return lse_cols

    def wrows(ref, c):
        return ref[wide(c), :]

    def add_to(ref, c, value):
        if c == 0:
            ref[...] = value
        else:
            ref[...] += value

    def expert_in(c):
        x = arrived(A, c)
        add_to(gate, c, nn(x, wrows(wg, c)))
        add_to(up, c, nn(x, wrows(wu, c)))

    def expert_cot(c):
        add_to(hgrad, c, nt(arrived(C, c), wd[:, wide(c)]))

    for t in range(chunks + 3):
        if t + 2 < chunks:
            kv_ready(t + 2)
            kv.send(1, t + 2)
            q_ready(t + 2)
            qb.send(1, t + 2)
        if t < chunks:
            kv.wait(1, t)
            kv.send(2, t)
            qb.wait(1, t)
            qb.send(2, t)
        if 0 <= t - 1 < chunks:
            kv.wait(2, t - 1)
            kv.send(3, t - 1)
            qb.wait(2, t - 1)
            qb.send(3, t - 1)
        if t == 1:
            w_loads[0].wait()
            w_loads[1].wait()
            w_loads[2].wait()
        if 0 <= t - 1 < chunks:
            expert_cot(t - 1)
        if 0 <= t - 2 < chunks:
            c = t - 2
            kv.wait(3, c)
            lse_cols = attend(c, lse_cols)
            send_out(A, c, nn(pick[...], att[c]), True)
        if 0 <= t - 3 < chunks:
            expert_in(t - 3)

    lse_t = lse_cols.T[0:HEADS]
    lsw[0] = lse_t
    stat_to = [None, ctx_peers[3], ctx_peers[4], ctx_peers[5]]

    def ls_copy(w):
        return pltpu.make_async_remote_copy(
            src_ref=lsw.at[WIN - 1 + w], dst_ref=lsw.at[w],
            send_sem=ls_send.at[w - 1], recv_sem=ls_recv.at[w - 1],
            device_id={"ctx": stat_to[w]}, device_id_type=MESH,
        )

    for w in range(1, WIN):
        lsw[WIN - 1 + w] = lse_t - hidden_by[w - 1]
        ls_copy(w).start()

    g, u, hg = gate[...], up[...], hgrad[...]
    sig = 1.0 / (1.0 + jnp.exp(-g))
    a = g * sig
    su = sig * (1.0 + g * (1.0 - sig)) * u
    act[...] = a
    slope_up[...] = su
    hidden = (a * u).astype(BF16)
    gate_grad = (hg * su).astype(BF16)
    up_grad = (hg * a).astype(BF16)
    for c in range(chunks):
        send_out(G, c, nt(gate_grad, wrows(wg, c)) + nt(up_grad, wrows(wu, c)), False)
    for c in range(chunks):
        send_out(O, c, nn(hidden, wd[:, wide(c)]), False)

    def dl_copy(w, c):
        return pltpu.make_async_remote_copy(
            src_ref=dlw.at[0, c], dst_ref=dlw.at[w, c],
            send_sem=dl_send.at[w - 1, c], recv_sem=dl_recv.at[w - 1, c],
            device_id={"ctx": stat_to[w]}, device_id_type=MESH,
        )

    def cot_back(c):
        x = nn(place[...], arrived(G, c)) * route_w + cot[c].astype(F32)
        new = x.astype(BF16)
        deltas = []
        cols_of = jnp.zeros((rows, 128), F32)
        for j in range(per):
            mine = new[:, span(j)]
            cw[0, c, j] = mine
            d = jnp.sum(mine.astype(F32) * att[c, :, span(j)].astype(F32), axis=1, keepdims=True)
            deltas.append(d)
            cols_of = jnp.where(lane_w == j, d, cols_of)
        dlw[0, c] = cols_of.T[0:8]
        cb.send(1, c)
        for w in range(1, WIN):
            dl_copy(w, c).start()
        for j in range(per):
            h = c * per + j
            keys = jnp.concatenate([kvw[w, c, 0, j] for w in range(WIN)], axis=0)
            vals = jnp.concatenate([kvw[w, c, 1, j] for w in range(WIN)], axis=0)
            ds = (probs[h] * (nt(cw[0, c, j], vals) - deltas[j])).astype(BF16)
            gq = (nn(ds, keys) * scale).astype(BF16)
            gqs[c, :, span(j)] = gq
        pltpu.make_async_copy(gqs.at[c], gq_out.at[0, :, wide(c)], put.at[0]).start()

    def key_side(c):
        for w in range(1, WIN):
            dl_copy(w, c).wait_recv()
        for j in range(per):
            h = c * per + j
            k, v = kvw[0, c, 0, j], kvw[0, c, 1, j]
            qs = jnp.concatenate([qw[w, c, j] for w in range(WIN)], axis=0)
            cs = jnp.concatenate([cw[w, c, j] for w in range(WIN)], axis=0)
            lse = jnp.concatenate([lsw[w, h : h + 1, :] for w in range(WIN)], axis=1)
            dl = jnp.concatenate([dlw[w, c, j : j + 1, :] for w in range(WIN)], axis=1)
            s = nt(k, qs) * scale - lse
            s = jnp.concatenate([s[:, 0:rows] + bias_t[...], s[:, rows:]], axis=1)
            p = jnp.exp(s)
            ds = (p * (nt(v, cs) - dl)).astype(BF16)
            gk = (nn(ds, qs) * scale).astype(BF16)
            pb = p.astype(BF16)
            gv = nn(pb, cs).astype(BF16)
            gkv[c, 0, j] = gk
            gkv[c, 1, j] = gv
            ps = p * (nt(gk, qs) * scale)
            m2 = jnp.sum(ps, axis=0, keepdims=True)
            u = tn(jnp.concatenate([ps.astype(BF16), pb], axis=0), jnp.concatenate([v, gv], axis=0))
            us[WIN - 2, c, j] = u[(WIN - 1) * rows :].astype(BF16)
            for w in range(WIN - 1):
                uloc[w, c, j] = u[w * rows : (w + 1) * rows]
            for w in range(WIN):
                m2s[w, c, j : j + 1, :] = m2[:, w * rows : (w + 1) * rows]
        su_chain.send(WIN - 1, c)
        for w in range(1, WIN):
            m2_copy(w, c).start()
        for j in range(per):
            h = c * per + j
            pltpu.make_async_copy(gkv.at[c, 0, j], gk_out.at[0, :, span(h)], put.at[1]).start()
            pltpu.make_async_copy(gkv.at[c, 1, j], gv_out.at[0, :, span(h)], put.at[2]).start()

    def m2_copy(w, c):
        return pltpu.make_async_remote_copy(
            src_ref=m2s.at[w, c], dst_ref=m2r.at[w, c],
            send_sem=m2_send.at[w - 1, c], recv_sem=m2_recv.at[w - 1, c],
            device_id={"ctx": ctx_peers[w - 1]}, device_id_type=MESH,
        )

    def sum_on(w, c):
        su_chain.wait(w, c)
        us[w - 2, c] = (ur[w - 1, c].astype(F32) + uloc[w - 1, c]).astype(BF16)
        su_chain.send(w - 1, c)

    def query_side(c):
        for j in range(per):
            h = c * per + j
            keys = jnp.concatenate([kvw[w, c, 0, j] for w in range(WIN)], axis=0)
            vals = jnp.concatenate([kvw[w, c, 1, j] for w in range(WIN)], axis=0)
            p = probs[h]
            st = nt(gqs[c, :, span(j)], keys) * scale
            mean = jnp.sum(p * st, axis=1, keepdims=True)
            pt = (p * (st - mean)).astype(BF16)
            t1[c, :, span(j)] = nn(pt, vals)

    def tangent(c):
        su_chain.wait(1, c)
        for w in range(1, WIN):
            m2_copy(w, c).wait_recv()
        m2 = m2s[0, c] + m2r[1, c] + m2r[2, c] + m2r[3, c]
        for j in range(per):
            mean = jnp.sum(jnp.where(eye, m2[j : j + 1, :], 0.0), axis=1, keepdims=True)
            u = ur[0, c, j].astype(F32) + uloc[0, c, j]
            tan[c, :, span(j)] = (t1[c, :, span(j)] + u - mean * att[c, :, span(j)].astype(F32)).astype(BF16)
        send_out(T, c, nn(pick[...], tan[c]), True)

    def layer(c):
        x = nn(place[...], arrived(O, c)) * route_w + att[c].astype(F32)
        los[c] = x.astype(BF16)
        pltpu.make_async_copy(los.at[c], lo_out.at[0, :, wide(c)], put.at[3]).start()

    def expert_tan(c):
        x = arrived(T, c)
        add_to(gate, c, nn(x, wrows(wg, c)))
        add_to(up, c, nn(x, wrows(wu, c)))

    def within(c):
        return 0 <= c < chunks

    for t in range(chunks + 7):
        if within(t - 5):
            sum_on(2, t - 5)
        if within(t - 4):
            sum_on(3, t - 4)
        if within(t - 2):
            cb.wait(2, t - 2)
            cb.send(3, t - 2)
        if within(t - 1):
            cb.wait(1, t - 1)
            cb.send(2, t - 1)
            qb.wait(3, t - 1)
        if within(t):
            cot_back(t)
        if t == 2:
            for w in range(1, WIN):
                ls_copy(w).wait_recv()
        if within(t - 3):
            cb.wait(3, t - 3)
            key_side(t - 3)
        if within(t - 6):
            tangent(t - 6)
        if within(t - 4):
            query_side(t - 4)
        if within(t - 4):
            layer(t - 4)
        if within(t - 7):
            expert_tan(t - 7)

    ht = (slope_up[...] * gate[...] + act[...] * up[...]).astype(BF16)
    for c in range(chunks):
        send_out(E, c, nn(ht, wd[:, wide(c)]), False)
    for c in range(chunks):
        x = nn(place[...], arrived(E, c)) * route_w + tan[c].astype(F32)
        tos[c] = x.astype(BF16)
        pltpu.make_async_copy(tos.at[c], to_out.at[0, :, wide(c)], put.at[4]).start()

    for chain in (kv, su_chain, qb, cb):
        chain.finish()
    for w in range(1, WIN):
        ls_copy(w).wait_send()
        for c in range(chunks):
            dl_copy(w, c).wait_send()
            m2_copy(w, c).wait_send()
    for kind in range(6):
        part = sends.at[kind, 1:n_exp]
        pltpu.make_async_copy(part, part, a2a_send.at[kind]).wait()
    pltpu.make_async_copy(gqs, gqs, put.at[0]).wait()
    for i in range(2):
        pltpu.make_async_copy(gkv.at[:, i], gkv.at[:, i], put.at[1 + i]).wait()
    pltpu.make_async_copy(los, los, put.at[3]).wait()
    pltpu.make_async_copy(tos, tos, put.at[4]).wait()


def hand_over(*refs):
    ins, outs, bufs, got, put = refs[:5], refs[5:10], refs[10:15], refs[15], refs[16]
    takes = [pltpu.make_async_copy(a, b, got.at[i]) for i, (a, b) in enumerate(zip(ins, bufs))]
    gives = [pltpu.make_async_copy(b, o, put.at[i]) for i, (b, o) in enumerate(zip(bufs, outs))]
    for copy in takes:
        copy.start()
    for take, give in zip(takes, gives):
        take.wait()
        give.start()
    for give in gives:
        give.wait()


def local(n_ctx, n_exp, query, key, value, cotangent, route_ids, route_weights, block_mask, w_gate, w_up, w_down):
    rows, model = query.shape[1:]
    ffh = w_gate.shape[2]
    width = model // HEADS
    per = HEADS // CHUNKS
    cols = per * width
    cap = 2 * rows // n_exp
    slots = n_exp * cap
    hbm = pl.BlockSpec(memory_space=pl.ANY)
    vmem = pl.BlockSpec(memory_space=pltpu.VMEM)
    dma = pltpu.SemaphoreType.DMA
    scratch = [
        pltpu.VMEM((WIN, CHUNKS, 2, per, rows, width), BF16),
        pltpu.VMEM((WIN, CHUNKS, per, rows, width), BF16),
        pltpu.VMEM((WIN, CHUNKS, per, rows, width), BF16),
        pltpu.VMEM((CHUNKS, 2, per, rows, width), BF16),
        pltpu.VMEM((WIN - 1, CHUNKS, per, rows, width), BF16),
        pltpu.VMEM((WIN - 1, CHUNKS, per, rows, width), BF16),
        pltpu.VMEM((WIN - 1, CHUNKS, per, rows, width), F32),
        pltpu.VMEM((CHUNKS, rows, cols), F32),
        pltpu.VMEM((WIN, CHUNKS, 8, rows), F32),
        pltpu.VMEM((WIN, CHUNKS, 8, rows), F32),
        pltpu.VMEM((2 * WIN - 1, HEADS, rows), F32),
        pltpu.VMEM((WIN, CHUNKS, 8, rows), F32),
        pltpu.VMEM((HEADS, rows, WIN * rows), F32),
        pltpu.VMEM((rows, WIN * rows), F32),
        pltpu.VMEM((rows, rows), F32),
        pltpu.VMEM((CHUNKS, rows, cols), BF16),
        pltpu.VMEM((CHUNKS, rows, cols), BF16),
        pltpu.VMEM((CHUNKS, rows, cols), BF16),
        pltpu.VMEM((CHUNKS, rows, cols), BF16),
        pltpu.VMEM((CHUNKS, rows, cols), BF16),
        pltpu.VMEM((CHUNKS, rows, cols), BF16),
        pltpu.VMEM((WIN - 1, CHUNKS, per, rows, width), BF16),
        pltpu.VMEM((model, ffh), BF16),
        pltpu.VMEM((model, ffh), BF16),
        pltpu.VMEM((ffh, model), BF16),
        pltpu.VMEM((slots, rows), BF16),
        pltpu.VMEM((rows, slots), BF16),
        pltpu.VMEM((6, n_exp, CHUNKS, cap, cols), BF16),
        pltpu.VMEM((6, n_exp, CHUNKS, cap, cols), BF16),
        pltpu.VMEM((slots, ffh), F32),
        pltpu.VMEM((slots, ffh), F32),
        pltpu.VMEM((slots, ffh), F32),
        pltpu.VMEM((slots, ffh), F32),
        pltpu.VMEM((slots, ffh), F32),
        dma((CHUNKS,)), dma((CHUNKS,)), dma((CHUNKS,)), dma((3,)), dma((5,)),
        dma((4,)),
        dma((WIN - 1, CHUNKS)), dma((WIN - 1, CHUNKS)), dma((WIN - 1, CHUNKS)), dma((WIN - 1, CHUNKS)),
        dma((WIN - 1, CHUNKS)), dma((WIN - 1, CHUNKS)), dma((WIN - 1, CHUNKS)),
        dma((WIN - 1,)), dma((WIN - 1,)), dma((WIN - 1, CHUNKS)), dma((WIN - 1, CHUNKS)),
        dma((6,)), dma((6, CHUNKS)),
    ]
    out = jax.ShapeDtypeStruct((1, rows, model), BF16)
    results = pl.pallas_call(
        functools.partial(kernel, n_ctx, n_exp),
        out_shape=(out,) * 5,
        in_specs=[hbm] * 4 + [vmem] * 3 + [hbm] * 3,
        out_specs=(hbm,) * 5,
        scratch_shapes=scratch,
        compiler_params=pltpu.CompilerParams(
            collective_id=0, has_side_effects=True, vmem_limit_bytes=60 * 1024 * 1024
        ),
    )(
        query, key, value, cotangent, route_ids.reshape(1, 1, rows), route_weights.reshape(1, 1, rows),
        block_mask, w_gate, w_up, w_down,
    )
    return pl.pallas_call(
        hand_over,
        out_shape=(out,) * 5,
        in_specs=[hbm] * 5,
        out_specs=(hbm,) * 5,
        scratch_shapes=[pltpu.VMEM((1, rows, model), BF16)] * 5 + [dma((5,)), dma((5,))],
    )(*results)


def solution(mesh):
    n_ctx, n_exp = mesh.shape["ctx"], mesh.shape["exp"]
    rows = P("exp", "ctx", None)
    weights = P("exp", None, None)
    return jax.shard_map(
        functools.partial(local, n_ctx, n_exp),
        mesh=mesh,
        in_specs=(rows,) * 7 + (weights,) * 3,
        out_specs=(rows,) * 5,
        check_vma=False,
    )
```

```python
import functools

import jax
import jax.numpy as jnp
from jax import lax
from jax.experimental import pallas as pl
from jax.experimental.pallas import tpu as pltpu
from jax.sharding import PartitionSpec as P

HEADS = 16
WIN = 4
CHUNKS = 4
O_LATE = True
G_AHEAD = 2
C_AHEAD = 4
MESH = pl.DeviceIdType.MESH
BF16 = jnp.bfloat16
F32 = jnp.float32
HIDE = -1e30


def nn(a, b):
    return lax.dot_general(a, b, (((1,), (0,)), ((), ())), preferred_element_type=F32)


def tn(a, b):
    return lax.dot_general(a, b, (((0,), (0,)), ((), ())), preferred_element_type=F32)


def nt(a, b):
    return lax.dot_general(a, b, (((1,), (1,)), ((), ())), preferred_element_type=F32)


def kernel(
    n_ctx, n_exp,
    q_in, k_in, v_in, c_in, ids_in, rw_in, mask_in, wg_in, wu_in, wd_in,
    lo_out, gq_out, gk_out, gv_out, to_out,
    kvw, qw, cw, gkv, us, ur, uloc, t1, m2s, m2r, lsw, dlw, probs, bias, bias_t, att, cot, gqs, tan, los, tos, kvr,
    wg, wu, wd, hid, pick, place,
    sends, recvs, gate, up, hgrad, slope_up, act,
    load_kv, load_q, load_c, load_w, put,
    ring_send, kv_recv, q_recv, c_recv, u_recv, kv_relay, m2_send, m2_recv, ls_send, ls_recv, dl_send, dl_recv,
    a2a_send, a2a_recv,
):
    chunks, per = kvw.shape[1], kvw.shape[3]
    rows, width = kvw.shape[4], kvw.shape[5]
    cols = per * width
    cap = sends.shape[3]
    scale = width ** -0.5
    me = lax.axis_index("ctx")
    expert = lax.axis_index("exp")

    def span(h):
        return slice(h * width, (h + 1) * width)

    def wide(c):
        return slice(c * cols, (c + 1) * cols)

    def kv_loads(c):
        out = []
        for j in range(per):
            out.append(pltpu.make_async_copy(k_in.at[0, :, span(c * per + j)], kvw.at[0, c, 0, j], load_kv.at[c]))
            out.append(pltpu.make_async_copy(v_in.at[0, :, span(c * per + j)], kvw.at[0, c, 1, j], load_kv.at[c]))
        return out

    def q_loads(c):
        return [pltpu.make_async_copy(q_in.at[0, :, span(c * per + j)], qw.at[0, c, j], load_q.at[c]) for j in range(per)]

    c_loads = [pltpu.make_async_copy(c_in.at[0, :, wide(c)], cot.at[c], load_c.at[c]) for c in range(chunks)]
    w_loads = [
        pltpu.make_async_copy(wd_in.at[0], wd, load_w.at[0]),
        pltpu.make_async_copy(wg_in.at[0], wg, load_w.at[1]),
        pltpu.make_async_copy(wu_in.at[0], wu, load_w.at[2]),
    ]
    for c in range(chunks):
        for copy in kv_loads(c) + q_loads(c):
            copy.start()
        c_loads[c].start()
    for copy in w_loads:
        copy.start()

    barrier = pltpu.get_barrier_semaphore()
    ctx_peers = [lax.rem(me + by + n_ctx, n_ctx) for by in (1, 2, 3, -1, -2, -3)]
    half, last = n_ctx // 2, n_ctx - 1
    far_peers = [lax.rem(me + by, n_ctx) for by in (half, half - 1, half + 1)]
    exp_peers = [lax.rem(expert + r, n_exp) for r in range(n_exp)]
    exp_back = [lax.rem(expert - r + n_exp, n_exp) for r in range(n_exp)]
    for peer in ctx_peers + far_peers:
        pl.semaphore_signal(barrier, inc=1, device_id={"ctx": peer}, device_id_type=MESH)
    for peer in exp_peers[1:]:
        pl.semaphore_signal(barrier, inc=1, device_id={"exp": peer}, device_id_type=MESH)

    lane = lax.broadcasted_iota(jnp.int32, (rows, 128), 1)
    eye = lax.broadcasted_iota(jnp.int32, (rows, rows), 0) == lax.broadcasted_iota(jnp.int32, (rows, rows), 1)
    ids = jnp.sum(jnp.where(eye, ids_in[0].astype(F32), 0.0), axis=1, keepdims=True).astype(jnp.int32)
    hot = (lane == ids).astype(F32)
    earlier = (
        lax.broadcasted_iota(jnp.int32, (rows, rows), 0) > lax.broadcasted_iota(jnp.int32, (rows, rows), 1)
    ).astype(BF16)
    rank = jnp.sum(nn(earlier, hot.astype(BF16)) * hot, axis=1, keepdims=True)
    ahead = ids - expert
    ahead = jnp.where(ahead < 0, ahead + n_exp, ahead)
    slot = ahead.astype(F32) * cap + rank
    slots = n_exp * cap
    slot_lane = lax.broadcasted_iota(jnp.int32, (rows, slots), 1).astype(F32)
    place_f = (slot_lane == slot).astype(F32)
    place[...] = place_f.astype(BF16)
    pick[...] = place_f.T.astype(BF16)
    route_w = jnp.sum(jnp.where(eye, rw_in[0], 0.0), axis=1, keepdims=True)

    qpos = lax.broadcasted_iota(jnp.int32, (rows, rows), 0)
    kpos = lax.broadcasted_iota(jnp.int32, (rows, rows), 1)
    bias[:, 0:rows] = jnp.where(qpos >= kpos, 0.0, HIDE)
    bias_t[...] = jnp.where(kpos >= qpos, 0.0, HIDE)
    hidden_by = []
    for w in range(1, WIN):
        seen = mask_in[0, :, w - 1 : w] * jnp.where(me >= w, 1, 0)
        cut = jnp.where(seen == 1, 0.0, HIDE)
        hidden_by.append(cut)
        bias[:, w * rows : (w + 1) * rows] = jnp.broadcast_to(cut, (rows, rows))

    pl.semaphore_wait(barrier, len(ctx_peers) + len(far_peers) + n_exp - 1)

    def hop(buf, send_sem, recv_sem, peer, w, c):
        return pltpu.make_async_remote_copy(
            src_ref=buf.at[w - 1, c], dst_ref=buf.at[w, c],
            send_sem=send_sem, recv_sem=recv_sem.at[w - 1, c],
            device_id={"ctx": peer}, device_id_type=MESH,
        )

    nxt, prv = ctx_peers[0], ctx_peers[3]

    class Forward:
        def __init__(self, buf, relay, send_sem, recv_sem, relay_sem):
            self.buf, self.relay, self.send_sem, self.recv_sem, self.relay_sem = buf, relay, send_sem, recv_sem, relay_sem

        def copy(self, src, dst, recv_sem, peer):
            return pltpu.make_async_remote_copy(
                src_ref=src, dst_ref=dst, send_sem=self.send_sem, recv_sem=recv_sem,
                device_id={"ctx": peer}, device_id_type=MESH,
            )

        def send(self, w, c):
            src, dst = self.buf.at[w - 1, c], self.buf.at[w, c]
            sem = self.recv_sem.at[w - 1, c]

            @pl.when((me < last) & (me != half - 1))
            def _():
                self.copy(src, dst, sem, nxt).start()

            @pl.when(me == half - 1)
            def _():
                self.copy(src.at[1], self.relay.at[w - 1, c], self.relay_sem.at[w - 1, c], last).start()
                self.copy(src.at[0], dst.at[0], sem, half).start()

        def wait(self, w, c):
            @pl.when(me == last)
            def _():
                part = self.relay.at[w - 1, c]
                pltpu.make_async_copy(part, part, self.relay_sem.at[w - 1, c]).wait()
                self.copy(part, self.buf.at[w, c, 1], self.recv_sem.at[w - 1, c], half).start()

            @pl.when(me > 0)
            def _():
                part = self.buf.at[w, c]
                pltpu.make_async_copy(part, part, self.recv_sem.at[w - 1, c]).wait()

        def finish(self):
            @pl.when(me < last)
            def _():
                pltpu.make_async_copy(self.buf.at[1:WIN], self.buf.at[1:WIN], self.send_sem).wait()

            @pl.when(me == last)
            def _():
                pltpu.make_async_copy(self.relay, self.relay, self.send_sem).wait()

    class Backward:
        def __init__(self, buf, send_sem, recv_sem):
            self.buf, self.send_sem, self.recv_sem = buf, send_sem, recv_sem

        def send(self, w, c):
            @pl.when(me > 0)
            def _():
                hop(self.buf, self.send_sem, self.recv_sem, prv, w, c).start()

        def wait(self, w, c):
            @pl.when(me < last)
            def _():
                hop(self.buf, self.send_sem, self.recv_sem, prv, w, c).wait_recv()

        def finish(self):
            @pl.when(me > 0)
            def _():
                pltpu.make_async_copy(self.buf.at[1:WIN], self.buf.at[1:WIN], self.send_sem).wait()

    kv = Forward(kvw, kvr, ring_send.at[0], kv_recv, kv_relay)

    class Sums:
        def copy(self, w, c):
            return pltpu.make_async_remote_copy(
                src_ref=us.at[w - 1, c], dst_ref=ur.at[w - 1, c], send_sem=ring_send.at[3], recv_sem=u_recv.at[w - 1, c],
                device_id={"ctx": nxt}, device_id_type=MESH,
            )

        def send(self, w, c):
            @pl.when(me < last)
            def _():
                self.copy(w, c).start()

        def wait(self, w, c):
            @pl.when(me > 0)
            def _():
                self.copy(w, c).wait_recv()

        def finish(self):
            @pl.when(me < last)
            def _():
                pltpu.make_async_copy(us, us, ring_send.at[3]).wait()

    su_chain = Sums()
    qb = Backward(qw, ring_send.at[1], q_recv)
    cb = Backward(cw, ring_send.at[2], c_recv)

    m2s[...] = jnp.zeros(m2s.shape, F32)

    @pl.when(me == 0)
    def _():
        kvw[1:WIN] = jnp.zeros((WIN - 1,) + kvw.shape[1:], BF16)
        ur[...] = jnp.zeros(ur.shape, BF16)

    @pl.when(me == last)
    def _():
        qw[1:WIN] = jnp.zeros((WIN - 1,) + qw.shape[1:], BF16)
        cw[1:WIN] = jnp.zeros((WIN - 1,) + cw.shape[1:], BF16)

    def exchange(kind, c, forward):
        peers = exp_peers if forward else exp_back
        return [
            pltpu.make_async_remote_copy(
                src_ref=sends.at[kind, r, c], dst_ref=recvs.at[kind, r, c],
                send_sem=a2a_send.at[kind], recv_sem=a2a_recv.at[kind, c],
                device_id={"exp": peers[r]}, device_id_type=MESH,
            )
            for r in range(1, n_exp)
        ]

    def send_out(kind, c, value, forward):
        parts = value.astype(BF16).reshape(n_exp, cap, cols)
        sends[kind, :, c] = parts
        recvs[kind, 0, c] = parts[0]
        for copy in exchange(kind, c, forward):
            copy.start()

    def arrived(kind, c):
        pltpu.make_async_copy(
            sends.at[kind, 1:n_exp, c], recvs.at[kind, 1:n_exp, c], a2a_recv.at[kind, c]
        ).wait()
        return recvs[kind, :, c].reshape(slots, cols)

    A, C, O, G, T, E = range(6)

    def kv_ready(c):
        pltpu.make_async_copy(kvw.at[0, c], kvw.at[0, c], load_kv.at[c]).wait()

    def q_ready(c):
        pltpu.make_async_copy(qw.at[0, c], qw.at[0, c], load_q.at[c]).wait()

    for c in range(min(2, chunks)):
        kv_ready(c)
        kv.send(1, c)
        q_ready(c)
        qb.send(1, c)
    def send_cot(c):
        c_loads[c].wait()
        send_out(C, c, nn(pick[...], cot[c]), True)

    for c in range(min(C_AHEAD, chunks)):
        send_cot(c)

    lane_w = lax.broadcasted_iota(jnp.int32, (rows, 128), 1)
    lse_cols = jnp.zeros((rows, 128), F32)

    def attend(c, lse_cols):
        for j in range(per):
            h = c * per + j
            keys = jnp.concatenate([kvw[w, c, 0, j] for w in range(WIN)], axis=0)
            vals = jnp.concatenate([kvw[w, c, 1, j] for w in range(WIN)], axis=0)
            s = nt(qw[0, c, j], keys) * scale + bias[...]
            top = jnp.max(s, axis=1, keepdims=True)
            e = jnp.exp(s - top)
            total = jnp.sum(e, axis=1, keepdims=True)
            p = e * (1.0 / total)
            probs[h] = p
            lse_cols = jnp.where(lane_w == h, top + jnp.log(total), lse_cols)
            att[c, :, span(j)] = nn(p.astype(BF16), vals).astype(BF16)
        return lse_cols

    def wrows(ref, c):
        return ref[wide(c), :]

    def add_to(ref, c, value):
        if c == 0:
            ref[...] = value
        else:
            ref[...] += value

    def expert_in(c):
        x = arrived(A, c)
        add_to(gate, c, nn(x, wrows(wg, c)))
        add_to(up, c, nn(x, wrows(wu, c)))

    def expert_cot(c):
        add_to(hgrad, c, nt(arrived(C, c), wd[:, wide(c)]))

    for t in range(chunks + 3):
        if t + 2 < chunks:
            kv_ready(t + 2)
            kv.send(1, t + 2)
            q_ready(t + 2)
            qb.send(1, t + 2)
        if C_AHEAD <= t + C_AHEAD < chunks:
            send_cot(t + C_AHEAD)
        if t < chunks:
            kv.wait(1, t)
            kv.send(2, t)
            qb.wait(1, t)
            qb.send(2, t)
        if 0 <= t - 1 < chunks:
            kv.wait(2, t - 1)
            kv.send(3, t - 1)
            qb.wait(2, t - 1)
            qb.send(3, t - 1)
        if t == 1:
            w_loads[0].wait()
            w_loads[1].wait()
            w_loads[2].wait()
        if 0 <= t - 1 < chunks:
            expert_cot(t - 1)
        if 0 <= t - 2 < chunks:
            c = t - 2
            kv.wait(3, c)
            lse_cols = attend(c, lse_cols)
            send_out(A, c, nn(pick[...], att[c]), True)
        if 0 <= t - 3 < chunks:
            expert_in(t - 3)

    lse_t = lse_cols.T[0:HEADS]
    lsw[0] = lse_t
    stat_to = [None, ctx_peers[3], ctx_peers[4], ctx_peers[5]]

    def ls_copy(w):
        return pltpu.make_async_remote_copy(
            src_ref=lsw.at[WIN - 1 + w], dst_ref=lsw.at[w],
            send_sem=ls_send.at[w - 1], recv_sem=ls_recv.at[w - 1],
            device_id={"ctx": stat_to[w]}, device_id_type=MESH,
        )

    for w in range(1, WIN):
        lsw[WIN - 1 + w] = lse_t - hidden_by[w - 1]
        ls_copy(w).start()

    g, u, hg = gate[...], up[...], hgrad[...]
    sig = 1.0 / (1.0 + jnp.exp(-g))
    a = g * sig
    su = sig * (1.0 + g * (1.0 - sig)) * u
    act[...] = a
    slope_up[...] = su
    hid[0] = (a * u).astype(BF16)
    hid[1] = (hg * su).astype(BF16)
    hid[2] = (hg * a).astype(BF16)

    def send_grad(c):
        send_out(G, c, nt(hid[1], wrows(wg, c)) + nt(hid[2], wrows(wu, c)), False)

    def send_forward(c):
        send_out(O, c, nn(hid[0], wd[:, wide(c)]), False)

    for c in range(min(G_AHEAD, chunks)):
        send_grad(c)
    if not O_LATE:
        for c in range(chunks):
            send_forward(c)

    def dl_copy(w, c):
        return pltpu.make_async_remote_copy(
            src_ref=dlw.at[0, c], dst_ref=dlw.at[w, c],
            send_sem=dl_send.at[w - 1, c], recv_sem=dl_recv.at[w - 1, c],
            device_id={"ctx": stat_to[w]}, device_id_type=MESH,
        )

    def cot_back(c):
        x = nn(place[...], arrived(G, c)) * route_w + cot[c].astype(F32)
        if c + G_AHEAD < chunks:
            send_grad(c + G_AHEAD)
        new = x.astype(BF16)
        deltas = []
        cols_of = jnp.zeros((rows, 128), F32)
        for j in range(per):
            mine = new[:, span(j)]
            cw[0, c, j] = mine
            d = jnp.sum(mine.astype(F32) * att[c, :, span(j)].astype(F32), axis=1, keepdims=True)
            deltas.append(d)
            cols_of = jnp.where(lane_w == j, d, cols_of)
        dlw[0, c] = cols_of.T[0:8]
        cb.send(1, c)
        for w in range(1, WIN):
            dl_copy(w, c).start()
        for j in range(per):
            h = c * per + j
            keys = jnp.concatenate([kvw[w, c, 0, j] for w in range(WIN)], axis=0)
            vals = jnp.concatenate([kvw[w, c, 1, j] for w in range(WIN)], axis=0)
            ds = (probs[h] * (nt(cw[0, c, j], vals) - deltas[j])).astype(BF16)
            gq = (nn(ds, keys) * scale).astype(BF16)
            gqs[c, :, span(j)] = gq
        pltpu.make_async_copy(gqs.at[c], gq_out.at[0, :, wide(c)], put.at[0]).start()

    def key_side(c):
        for w in range(1, WIN):
            dl_copy(w, c).wait_recv()
        for j in range(per):
            h = c * per + j
            k, v = kvw[0, c, 0, j], kvw[0, c, 1, j]
            qs = jnp.concatenate([qw[w, c, j] for w in range(WIN)], axis=0)
            cs = jnp.concatenate([cw[w, c, j] for w in range(WIN)], axis=0)
            lse = jnp.concatenate([lsw[w, h : h + 1, :] for w in range(WIN)], axis=1)
            dl = jnp.concatenate([dlw[w, c, j : j + 1, :] for w in range(WIN)], axis=1)
            s = nt(k, qs) * scale - lse
            s = jnp.concatenate([s[:, 0:rows] + bias_t[...], s[:, rows:]], axis=1)
            p = jnp.exp(s)
            ds = (p * (nt(v, cs) - dl)).astype(BF16)
            gk = (nn(ds, qs) * scale).astype(BF16)
            pb = p.astype(BF16)
            gv = nn(pb, cs).astype(BF16)
            gkv[c, 0, j] = gk
            gkv[c, 1, j] = gv
            ps = p * (nt(gk, qs) * scale)
            m2 = jnp.sum(ps, axis=0, keepdims=True)
            u = tn(jnp.concatenate([ps.astype(BF16), pb], axis=0), jnp.concatenate([v, gv], axis=0))
            us[WIN - 2, c, j] = u[(WIN - 1) * rows :].astype(BF16)
            for w in range(WIN - 1):
                uloc[w, c, j] = u[w * rows : (w + 1) * rows]
            for w in range(WIN):
                m2s[w, c, j : j + 1, :] = m2[:, w * rows : (w + 1) * rows]
        su_chain.send(WIN - 1, c)
        for w in range(1, WIN):
            m2_copy(w, c).start()
        for j in range(per):
            h = c * per + j
            pltpu.make_async_copy(gkv.at[c, 0, j], gk_out.at[0, :, span(h)], put.at[1]).start()
            pltpu.make_async_copy(gkv.at[c, 1, j], gv_out.at[0, :, span(h)], put.at[2]).start()

    def m2_copy(w, c):
        return pltpu.make_async_remote_copy(
            src_ref=m2s.at[w, c], dst_ref=m2r.at[w, c],
            send_sem=m2_send.at[w - 1, c], recv_sem=m2_recv.at[w - 1, c],
            device_id={"ctx": ctx_peers[w - 1]}, device_id_type=MESH,
        )

    def sum_on(w, c):
        su_chain.wait(w, c)
        us[w - 2, c] = (ur[w - 1, c].astype(F32) + uloc[w - 1, c]).astype(BF16)
        su_chain.send(w - 1, c)

    def query_side(c):
        for j in range(per):
            h = c * per + j
            keys = jnp.concatenate([kvw[w, c, 0, j] for w in range(WIN)], axis=0)
            vals = jnp.concatenate([kvw[w, c, 1, j] for w in range(WIN)], axis=0)
            p = probs[h]
            st = nt(gqs[c, :, span(j)], keys) * scale
            mean = jnp.sum(p * st, axis=1, keepdims=True)
            pt = (p * (st - mean)).astype(BF16)
            t1[c, :, span(j)] = nn(pt, vals)

    def tangent(c):
        su_chain.wait(1, c)
        for w in range(1, WIN):
            m2_copy(w, c).wait_recv()
        m2 = m2s[0, c] + m2r[1, c] + m2r[2, c] + m2r[3, c]
        for j in range(per):
            mean = jnp.sum(jnp.where(eye, m2[j : j + 1, :], 0.0), axis=1, keepdims=True)
            u = ur[0, c, j].astype(F32) + uloc[0, c, j]
            tan[c, :, span(j)] = (t1[c, :, span(j)] + u - mean * att[c, :, span(j)].astype(F32)).astype(BF16)
        send_out(T, c, nn(pick[...], tan[c]), True)

    def layer(c):
        x = nn(place[...], arrived(O, c)) * route_w + att[c].astype(F32)
        los[c] = x.astype(BF16)
        pltpu.make_async_copy(los.at[c], lo_out.at[0, :, wide(c)], put.at[3]).start()

    def expert_tan(c):
        x = arrived(T, c)
        add_to(gate, c, nn(x, wrows(wg, c)))
        add_to(up, c, nn(x, wrows(wu, c)))

    def within(c):
        return 0 <= c < chunks

    for t in range(chunks + 7):
        if within(t - 5):
            sum_on(2, t - 5)
        if within(t - 4):
            sum_on(3, t - 4)
        if within(t - 2):
            cb.wait(2, t - 2)
            cb.send(3, t - 2)
        if within(t - 1):
            cb.wait(1, t - 1)
            cb.send(2, t - 1)
            qb.wait(3, t - 1)
        if within(t):
            cot_back(t)
        if t == 2:
            for w in range(1, WIN):
                ls_copy(w).wait_recv()
        if within(t - 3):
            cb.wait(3, t - 3)
            key_side(t - 3)
            if O_LATE:
                send_forward(t - 3)
        if within(t - 6):
            tangent(t - 6)
        if within(t - 4):
            query_side(t - 4)
        if within(t - 4) and not O_LATE:
            layer(t - 4)
        if within(t - 7):
            expert_tan(t - 7)

    ht = (slope_up[...] * gate[...] + act[...] * up[...]).astype(BF16)
    for c in range(chunks):
        send_out(E, c, nn(ht, wd[:, wide(c)]), False)
    if O_LATE:
        for c in range(chunks):
            layer(c)
    for c in range(chunks):
        x = nn(place[...], arrived(E, c)) * route_w + tan[c].astype(F32)
        tos[c] = x.astype(BF16)
        pltpu.make_async_copy(tos.at[c], to_out.at[0, :, wide(c)], put.at[4]).start()

    for chain in (kv, su_chain, qb, cb):
        chain.finish()
    for w in range(1, WIN):
        ls_copy(w).wait_send()
        for c in range(chunks):
            dl_copy(w, c).wait_send()
            m2_copy(w, c).wait_send()
    for kind in range(6):
        part = sends.at[kind, 1:n_exp]
        pltpu.make_async_copy(part, part, a2a_send.at[kind]).wait()
    pltpu.make_async_copy(gqs, gqs, put.at[0]).wait()
    for i in range(2):
        pltpu.make_async_copy(gkv.at[:, i], gkv.at[:, i], put.at[1 + i]).wait()
    pltpu.make_async_copy(los, los, put.at[3]).wait()
    pltpu.make_async_copy(tos, tos, put.at[4]).wait()


def hand_over(*refs):
    ins, outs, bufs, got, put = refs[:5], refs[5:10], refs[10:15], refs[15], refs[16]
    takes = [pltpu.make_async_copy(a, b, got.at[i]) for i, (a, b) in enumerate(zip(ins, bufs))]
    gives = [pltpu.make_async_copy(b, o, put.at[i]) for i, (b, o) in enumerate(zip(bufs, outs))]
    for copy in takes:
        copy.start()
    for take, give in zip(takes, gives):
        take.wait()
        give.start()
    for give in gives:
        give.wait()


def local(n_ctx, n_exp, query, key, value, cotangent, route_ids, route_weights, block_mask, w_gate, w_up, w_down):
    rows, model = query.shape[1:]
    ffh = w_gate.shape[2]
    width = model // HEADS
    per = HEADS // CHUNKS
    cols = per * width
    cap = 2 * rows // n_exp
    slots = n_exp * cap
    hbm = pl.BlockSpec(memory_space=pl.ANY)
    vmem = pl.BlockSpec(memory_space=pltpu.VMEM)
    dma = pltpu.SemaphoreType.DMA
    scratch = [
        pltpu.VMEM((WIN, CHUNKS, 2, per, rows, width), BF16),
        pltpu.VMEM((WIN, CHUNKS, per, rows, width), BF16),
        pltpu.VMEM((WIN, CHUNKS, per, rows, width), BF16),
        pltpu.VMEM((CHUNKS, 2, per, rows, width), BF16),
        pltpu.VMEM((WIN - 1, CHUNKS, per, rows, width), BF16),
        pltpu.VMEM((WIN - 1, CHUNKS, per, rows, width), BF16),
        pltpu.VMEM((WIN - 1, CHUNKS, per, rows, width), F32),
        pltpu.VMEM((CHUNKS, rows, cols), F32),
        pltpu.VMEM((WIN, CHUNKS, 8, rows), F32),
        pltpu.VMEM((WIN, CHUNKS, 8, rows), F32),
        pltpu.VMEM((2 * WIN - 1, HEADS, rows), F32),
        pltpu.VMEM((WIN, CHUNKS, 8, rows), F32),
        pltpu.VMEM((HEADS, rows, WIN * rows), F32),
        pltpu.VMEM((rows, WIN * rows), F32),
        pltpu.VMEM((rows, rows), F32),
        pltpu.VMEM((CHUNKS, rows, cols), BF16),
        pltpu.VMEM((CHUNKS, rows, cols), BF16),
        pltpu.VMEM((CHUNKS, rows, cols), BF16),
        pltpu.VMEM((CHUNKS, rows, cols), BF16),
        pltpu.VMEM((CHUNKS, rows, cols), BF16),
        pltpu.VMEM((CHUNKS, rows, cols), BF16),
        pltpu.VMEM((WIN - 1, CHUNKS, per, rows, width), BF16),
        pltpu.VMEM((model, ffh), BF16),
        pltpu.VMEM((model, ffh), BF16),
        pltpu.VMEM((ffh, model), BF16),
        pltpu.VMEM((3, slots, ffh), BF16),
        pltpu.VMEM((slots, rows), BF16),
        pltpu.VMEM((rows, slots), BF16),
        pltpu.VMEM((6, n_exp, CHUNKS, cap, cols), BF16),
        pltpu.VMEM((6, n_exp, CHUNKS, cap, cols), BF16),
        pltpu.VMEM((slots, ffh), F32),
        pltpu.VMEM((slots, ffh), F32),
        pltpu.VMEM((slots, ffh), F32),
        pltpu.VMEM((slots, ffh), F32),
        pltpu.VMEM((slots, ffh), F32),
        dma((CHUNKS,)), dma((CHUNKS,)), dma((CHUNKS,)), dma((3,)), dma((5,)),
        dma((4,)),
        dma((WIN - 1, CHUNKS)), dma((WIN - 1, CHUNKS)), dma((WIN - 1, CHUNKS)), dma((WIN - 1, CHUNKS)),
        dma((WIN - 1, CHUNKS)), dma((WIN - 1, CHUNKS)), dma((WIN - 1, CHUNKS)),
        dma((WIN - 1,)), dma((WIN - 1,)), dma((WIN - 1, CHUNKS)), dma((WIN - 1, CHUNKS)),
        dma((6,)), dma((6, CHUNKS)),
    ]
    out = jax.ShapeDtypeStruct((1, rows, model), BF16)
    results = pl.pallas_call(
        functools.partial(kernel, n_ctx, n_exp),
        out_shape=(out,) * 5,
        in_specs=[hbm] * 4 + [vmem] * 3 + [hbm] * 3,
        out_specs=(hbm,) * 5,
        scratch_shapes=scratch,
        compiler_params=pltpu.CompilerParams(
            collective_id=0, has_side_effects=True, vmem_limit_bytes=60 * 1024 * 1024
        ),
    )(
        query, key, value, cotangent, route_ids.reshape(1, 1, rows), route_weights.reshape(1, 1, rows),
        block_mask, w_gate, w_up, w_down,
    )
    return pl.pallas_call(
        hand_over,
        out_shape=(out,) * 5,
        in_specs=[hbm] * 5,
        out_specs=(hbm,) * 5,
        scratch_shapes=[pltpu.VMEM((1, rows, model), BF16)] * 5 + [dma((5,)), dma((5,))],
    )(*results)


def solution(mesh):
    n_ctx, n_exp = mesh.shape["ctx"], mesh.shape["exp"]
    rows = P("exp", "ctx", None)
    weights = P("exp", None, None)
    return jax.shard_map(
        functools.partial(local, n_ctx, n_exp),
        mesh=mesh,
        in_specs=(rows,) * 7 + (weights,) * 3,
        out_specs=(rows,) * 5,
        check_vma=False,
    )
```
